256 devices in a mesh: bus: 64 (over y, z_lo, x), harm: 4 (over z_hi, core).
Axes of the slice: x: 4, y: 4, z: 8 (z_hi: 2, z_lo: 4; z = z_hi * 4 + z_lo), core: 2. Of those that a mesh axis runs over, the one named last changes fastest.
Arguments:
- injection: bfloat16 [64, 192, 32, 128], P('harm', 'bus'), may hold values from -6 to 6
- inv_diag: bfloat16 [64, 192, 128, 128], P('harm', 'bus'), may hold values from -0.5 to 0.5
- off_tiles: bfloat16 [64, 192, 3, 128, 128], P('harm', 'bus'), may hold values from -0.15625 to 0.15625
- pattern: int32 [192, 3], P('bus'), may hold values from 0 to 191, as said below
- coupling: bfloat16 [1024, 6, 64, 384], P('bus', None, 'harm'), may hold values from -0.15625 to 0.15625
- site_map: int32 [1024], P('bus'), may hold values from 0 to 63, as said below
- bus_map: int32 [1024], P('bus'), may hold values from 0 to 63
Outputs:
- voltage: float32 [64, 192, 32, 128], P('harm', 'bus')
The draws below stay inside these ranges and needn't reach their ends.
Inputs may be any that keep to these rules, and one draw needn't show every extreme that they name: `pattern`: each tile row has one column in its own site other than itself, and one in each neighbouring site, a second own one where no neighbour exists. `site_map`: the slot's own index of bus, or one of its two neighbours.
All inputs are finite; a program needn't handle non-finite values.
Results may differ from the reference program's by a relative error of at most 0.0037.
Values may be sent and summed in bfloat16 or wider, within the bound.
A program may use at most 64 MiB of HBM per device.

```python
import jax
import jax.numpy as jnp
from jax import lax

HARM = 64
SCEN = 32
TILE = 128
KOFF = 3
BLOCKS_DEV = 1
CONV_DEV = 16
ITERS = 2
TILES = 192
CONV = 1024
CIN = 384
N_BUS = 64


def draw_pattern(key, part):
    per_site = 3 * BLOCKS_DEV
    count = per_site * N_BUS
    first, second, third = jax.random.split(jax.random.fold_in(key, 11), 3)
    rows_all = jnp.arange(count, dtype=jnp.int32)
    site = rows_all // per_site
    within = rows_all % per_site
    own = site * per_site + (within + jax.random.randint(first, (count,), 1, per_site)) % per_site
    left_pick = jax.random.randint(second, (count,), 0, per_site)
    right_pick = jax.random.randint(third, (count,), 0, per_site)
    spare_left = site * per_site + (within + 1 + left_pick % (per_site - 1)) % per_site
    spare_right = site * per_site + (within + 1 + right_pick % (per_site - 1)) % per_site
    left = jnp.where(site > 0, (site - 1) * per_site + left_pick, spare_left)
    right = jnp.where(site < N_BUS - 1, (site + 1) * per_site + right_pick, spare_right)
    return jnp.stack([own, left, right], axis=1).astype(jnp.int32)


def draw_site_map(key, part):
    count = CONV_DEV * N_BUS
    slots = jnp.arange(count, dtype=jnp.int32) // CONV_DEV
    offset = jax.random.randint(jax.random.fold_in(key, 23), (count,), -1, 2)
    return jnp.clip(slots + offset, 0, N_BUS - 1).astype(jnp.int32)


def set_ends(entries, rng, least, largest):
    spot = [jax.random.randint(jax.random.fold_in(rng, axis), (), 0, length) for axis, length in enumerate(entries.shape)]
    main_axis = entries.shape.index(max(entries.shape))
    beside = spot[:main_axis] + [(spot[main_axis] + 1) % entries.shape[main_axis]] + spot[main_axis + 1:]
    return entries.at[tuple(spot)].set(least).at[tuple(beside)].set(largest)


def shard_levels(own_key, shape, cuts, low, largest):
    loudness, own = 1.0, jax.random.fold_in(own_key, 6)
    for axis_at, parts in cuts:
        steps = jnp.exp(jax.random.uniform(jax.random.fold_in(own, axis_at), (parts,), jnp.float32, low / len(cuts), largest / len(cuts)))
        loudness = loudness * jnp.repeat(steps, shape[axis_at] // parts).reshape([-1 if axis == axis_at else 1 for axis in range(len(shape))])
    return loudness


def bell_draw(stream_key, dims, scale, most, cuts=(), kind=jnp.bfloat16):
    values = scale * jax.random.normal(stream_key, dims, jnp.float32)
    if cuts:
        values = values * shard_levels(stream_key, dims, cuts, -0.22, 0.18)
    return jnp.clip(values, -most, most).astype(kind)


def setup_inputs(seed: int = 0) -> dict:
    arg_keys = jax.random.split(jax.random.key(seed), 8)
    injection = bell_draw(arg_keys[0], (HARM, TILES, SCEN, TILE), 1.0, 6.0, ((0, 4), (1, 64)))
    inv_diag = bell_draw(arg_keys[1], (HARM, TILES, TILE, TILE), TILE ** -0.5, 0.5, ((0, 4), (1, 64)))
    off_tiles = bell_draw(arg_keys[2], (HARM, TILES, KOFF, TILE, TILE), (4 * KOFF * TILE) ** -0.5, 0.15625, ((0, 4), (1, 64)))
    pattern = draw_pattern(jax.random.fold_in(arg_keys[7], 71), 0)
    coupling = bell_draw(arg_keys[4], (CONV, 6, HARM, CIN), (4 * CIN) ** -0.5, 0.15625, ((0, 64), (2, 4)))
    site_map = draw_site_map(jax.random.fold_in(arg_keys[7], 71), 0)
    bus_map = set_ends(jax.random.randint(arg_keys[6], (CONV,), 0, TILE // 2 * BLOCKS_DEV), jax.random.fold_in(arg_keys[6], 1), 0, (TILE // 2 * BLOCKS_DEV) - 1).astype(jnp.int32)
    return dict(injection=injection, inv_diag=inv_diag, off_tiles=off_tiles, pattern=pattern, coupling=coupling, site_map=site_map, bus_map=bus_map)


def tile_apply(arrays):
    left, right = arrays
    return jnp.einsum('tsa,tab->tsb', left.astype(jnp.float32), right.astype(jnp.float32))


def network_apply(arrays):
    columns, tiles = arrays
    return jnp.einsum('tksa,tkab->tsb', columns.astype(jnp.float32), tiles.astype(jnp.float32))


def reference(injection, inv_diag, off_tiles, pattern, coupling, site_map, bus_map):
    half = TILE // 2
    bus_block = (bus_map // half).astype(jnp.int32)
    bus_row = (bus_map % half).astype(jnp.int32)
    voltage = lax.map(tile_apply, (injection, inv_diag))
    for sweep in range(ITERS):
        rounded = voltage.astype(jnp.bfloat16)
        columns = rounded[:, pattern]
        network = lax.map(network_apply, (columns, off_tiles))
        grid = rounded.reshape(HARM, N_BUS, 3, BLOCKS_DEV, SCEN, 2, half).transpose(1, 3, 6, 4, 0, 5, 2)
        terminal = grid[site_map, bus_block, bus_row].reshape(CONV, SCEN, 6 * HARM)
        currents = jnp.einsum('csi,cohi->csoh', terminal.astype(jnp.float32), coupling.astype(jnp.float32)).astype(jnp.bfloat16)
        spread = currents.transpose(0, 1, 3, 2).reshape(CONV, SCEN, HARM, 2, 3).astype(jnp.float32)
        summed = jnp.zeros((N_BUS, BLOCKS_DEV, half, SCEN, HARM, 2, 3), jnp.float32).at[site_map, bus_block, bus_row].add(spread)
        injected = summed.transpose(4, 0, 6, 1, 3, 5, 2).reshape(HARM, N_BUS * 3 * BLOCKS_DEV, SCEN, TILE)
        residual = (injection.astype(jnp.float32) - network - injected).astype(jnp.bfloat16)
        voltage = lax.map(tile_apply, (residual, inv_diag))
    return voltage
```

```python
import functools

import jax
import jax.numpy as jnp
import numpy as np
from jax import lax
from jax.experimental import pallas as pl
from jax.experimental.pallas import tpu as pltpu
from jax.sharding import PartitionSpec as P

ITERS = 2
MESH = pl.DeviceIdType.MESH
F32 = jnp.float32
BF16 = jnp.bfloat16

X_L, X_R, V_L, V_R, T_SIB, T_PAR, T_FWD, Z_L, Z_R = range(9)
PER_SWEEP = 9


def dot(a, b):
    return jnp.dot(a, b, preferred_element_type=F32)


def block_swap(a, masks):
    out = a
    for k in range(1, 4):
        moved = pltpu.roll(pltpu.roll(a, 32 * k, 1), 8 - 2 * k, 0)
        out = jnp.where(masks[k], moved, out)
    return out


def kernel(
    n_bus,
    site_ref, bus_ref, pat_ref, order_ref, inj_hbm, inv_hbm, off_hbm, cpl_hbm,
    out_hbm,
    inj, inv, off, cpl, perm, bp, vb, win_0, win_1, tabs, ehot, hh, base, xs, xr, tta, ttb, cur, zz, spread, outv,
    load_sem, send_sem, recv_sem, tab_send, tab_recv, out_sem,
):
    win = (win_0, win_1)
    me = lax.axis_index("bus")
    harm = lax.axis_index("harm")
    left = lax.rem(me + n_bus - 1, n_bus)
    right = lax.rem(me + 1, n_bus)
    zh, core = harm // 2, lax.rem(harm, 2)
    to_left, to_right = (left, harm), (right, harm)
    sibling = (me, zh * 2 + 1 - core)
    partner = (me, (1 - zh) * 2 + core)

    loads = [
        pltpu.make_async_copy(src, dst, load_sem.at[i])
        for i, (src, dst) in enumerate(((inj_hbm, inj), (inv_hbm, inv), (cpl_hbm, cpl), (off_hbm, off)))
    ]
    for load in loads:
        load.start()

    barrier = pltpu.get_barrier_semaphore()
    for peer in (to_left, to_right, sibling, partner):
        pl.semaphore_signal(barrier, inc=1, device_id=peer, device_id_type=MESH)

    conv_row = lax.broadcasted_iota(jnp.int32, (32, 128), 0) // 2
    table = jnp.zeros((32, 128), jnp.int32)
    for c in range(16):
        table = jnp.where(conv_row == c, site_ref[c] * 128 + bus_ref[c], table)
    tabs[1] = table

    pl.semaphore_wait(barrier, 4)

    def remote(src, dst, send, recv, peer):
        return pltpu.make_async_remote_copy(
            src_ref=src, dst_ref=dst, send_sem=send, recv_sem=recv, device_id=peer, device_id_type=MESH
        )

    tab_copies = [
        remote(tabs.at[1], tabs.at[0], tab_send.at[0], tab_recv.at[0], to_right),
        remote(tabs.at[1], tabs.at[2], tab_send.at[1], tab_recv.at[1], to_left),
    ]
    for copy in tab_copies:
        copy.start()

    def sweep_copies(w):
        def one(slot, src, dst, peer):
            return remote(src, dst, send_sem.at[w * PER_SWEEP + slot], recv_sem.at[w * PER_SWEEP + slot], peer)

        return [
            one(X_L, xs.at[w, 0], xr.at[w, 1], to_left),
            one(X_R, xs.at[w, 2], xr.at[w, 0], to_right),
            one(V_L, vb.at[w], win[w].at[2], to_left),
            one(V_R, vb.at[w], win[w].at[0], to_right),
            one(T_SIB, tta.at[w, pl.ds(0, 96)], tta.at[w, pl.ds(96, 96)], sibling),
            one(T_PAR, tta.at[w, pl.ds(0, 96)], ttb.at[w, pl.ds(0, 96)], partner),
            one(T_FWD, ttb.at[w, pl.ds(0, 96)], ttb.at[w, pl.ds(96, 96)], sibling),
            one(Z_L, zz.at[w, 1], zz.at[w, 2], to_left),
            one(Z_R, zz.at[w, 1], zz.at[w, 0], to_right),
        ]

    loads[0].wait()
    loads[1].wait()

    def first(h, carry):
        for p in range(3):
            rounded = dot(inj[h, p], inv[h, p]).astype(BF16)
            vb[0, h, p] = rounded
            win[0][1, h, p] = rounded
        return carry

    lax.fori_loop(0, 16, first, 0, unroll=4)

    for copy in tab_copies:
        copy.wait()

    parity = lax.rem(lax.broadcasted_iota(jnp.int32, (32, 128), 0), 2)
    lane = lax.broadcasted_iota(jnp.int32, (32, 128), 1)
    row256 = lax.rem(lax.broadcasted_iota(jnp.int32, (32, 256), 0), 2)
    lane256 = lax.broadcasted_iota(jnp.int32, (32, 256), 1)
    bus256 = lax.rem(lane256, 64) + me * 128
    part256 = lane256 // 64
    for g in range(3):
        tab = tabs[g]
        hit = (tab + parity * 64) == (lane + me * 128)
        ehot[g * 32 : g * 32 + 32] = jnp.where(hit, 1.0, 0.0).astype(BF16)
        wide = jnp.concatenate([tab, tab], axis=1)
        for m in range(2):
            hit = (wide == bus256) & (part256 == row256 * 2 + m)
            at = g * 64 + m * 32
            hh[at : at + 32] = jnp.where(hit, 1.0, 0.0).astype(BF16)

    sub = lax.broadcasted_iota(jnp.int32, (8, 128), 0) // 2
    chunk = lax.broadcasted_iota(jnp.int32, (8, 128), 1) // 32
    shift = lax.rem(chunk - sub + 4, 4)
    masks = [shift == k for k in range(4)]
    chunk96 = lax.broadcasted_iota(jnp.int32, (96, 128), 1) // 32
    chunk_masks = [chunk96 == k for k in range(4)]

    links = []
    for p in range(3):
        at = [pat_ref[p, k] - (me - 1) * 3 for k in range(3)]
        own = [(a >= 3) & (a < 6) for a in at]
        k0 = jnp.where(own[0], 0, jnp.where(own[1], 1, 2))
        k1 = jnp.where(k0 == 0, 1, 0)
        k2 = jnp.where(k0 == 2, 1, 2)

        def pick(k):
            return jnp.where(k == 0, at[0], jnp.where(k == 1, at[1], at[2]))

        links.append((k0, jnp.clip(pick(k0) - 3, 0, 2), k1, jnp.clip(pick(k1), 0, 8), k2, jnp.clip(pick(k2), 0, 8)))

    for w in range(ITERS):
        copies = sweep_copies(w)
        for j in range(6):
            some = vb[w].reshape(1536, 128)[j * 256 : j * 256 + 256]
            got = lax.dot_general(
                ehot[...], some, (((1,), (1,)), ((), ())), preferred_element_type=F32
            ).astype(BF16)
            for g in range(3):
                xs[w, g, :, j * 256 : j * 256 + 256] = got[g * 32 : g * 32 + 32]
        for slot in (X_L, X_R, V_L, V_R):
            copies[slot].start()

        if w == 0:
            loads[2].wait()
            col = lax.broadcasted_iota(jnp.int32, (8, 512), 1)
            slot_bits = (col // 256) * 2 + jnp.where(lax.rem(col, 256) >= 96, 1, 0)
            source = jnp.bitwise_xor(slot_bits, harm) * 96 + order_ref[...]
            for r in range(48):
                row = lax.broadcasted_iota(jnp.int32, (8, 512), 0) + r * 8
                hot = jnp.where(row == source[0:1], 1.0, 0.0)
                if r % 2 == 0:
                    kept = hot
                else:
                    perm[(r - 1) * 8 : (r + 1) * 8] = jnp.concatenate([kept, hot], axis=0).astype(BF16)

            def permute(c, carry):
                rows = pl.ds(pl.multiple_of(c * 96, 96), 96)
                bp[rows] = dot(cpl[rows], perm[...]).astype(BF16)
                return carry

            lax.fori_loop(0, 16, permute, 0)

        copies[X_L].wait_recv()
        copies[X_R].wait_recv()
        for tp in range(6):
            for up in range(2):
                both = []
                for t in (2 * tp, 2 * tp + 1):
                    rows, lanes = slice(up * 16, up * 16 + 16), slice(t * 128, t * 128 + 128)
                    both.append(
                        xs[w, 1, rows, lanes].astype(F32)
                        + xr[w, 0, rows, lanes].astype(F32)
                        + xr[w, 1, rows, lanes].astype(F32)
                    )
                for half in range(2):
                    u = up * 2 + half
                    swapped = [block_swap(b[half * 8 : half * 8 + 8], masks) for b in both]
                    tta[w, tp * 16 : tp * 16 + 16, u * 128 : u * 128 + 128] = jnp.concatenate(
                        swapped, axis=0
                    ).astype(BF16)
        copies[T_PAR].start()
        copies[T_SIB].start()

        if w == 0:
            loads[3].wait()

        def own_links(h, carry):
            for p in range(3):
                k0, own_at = links[p][:2]
                base[h, p] = inj[h, p].astype(F32) - dot(vb[w, h, own_at], off[h, p, k0])
            return carry

        lax.fori_loop(0, 16, own_links, 0, unroll=4)

        def couple(held, at, add):
            for u in range(4):
                rhs = held[w, :, u * 128 : u * 128 + 128]
                total = None
                for q in range(4):
                    c = u * 4 + q
                    one = dot(bp[c * 96 : c * 96 + 96, at : at + 192], rhs)
                    total = one if total is None else jnp.where(chunk_masks[q], one, total)
                lanes = slice(u * 128, u * 128 + 128)
                cur[:, lanes] = cur[:, lanes] + total if add else total

        copies[T_SIB].wait_recv()
        couple(tta, 0, False)
        copies[T_PAR].wait_recv()
        copies[T_FWD].start()
        copies[T_FWD].wait_recv()
        couple(ttb, 256, True)

        for up in range(2):
            for j in range(12):
                m, ph = j // 6, j % 6
                swapped = [
                    block_swap(cur[j * 8 : j * 8 + 8, u * 128 : u * 128 + 128], masks)
                    for u in (2 * up, 2 * up + 1)
                ]
                at = m * 32 + up * 16
                zz[w, 1, at : at + 16, ph * 128 : ph * 128 + 128] = jnp.concatenate(
                    swapped, axis=0
                ).astype(BF16)
        copies[Z_L].start()
        copies[Z_R].start()

        copies[V_L].wait_recv()
        copies[V_R].wait_recv()

        def other_links(h, carry):
            for p in range(3):
                _, _, k1, at1, k2, at2 = links[p]
                columns = jnp.concatenate(
                    [win[w][at1 // 3, h, lax.rem(at1, 3)], win[w][at2 // 3, h, lax.rem(at2, 3)]], axis=1
                )
                tiles = jnp.concatenate([off[h, p, k1], off[h, p, k2]], axis=0)
                base[h, p] = base[h, p] - dot(columns, tiles)
            return carry

        lax.fori_loop(0, 16, other_links, 0, unroll=4)

        copies[Z_L].wait_recv()
        copies[Z_R].wait_recv()
        spread[...] = lax.dot_general(
            zz[w].reshape(192, 768), hh[...], (((0,), (0,)), ((), ())), preferred_element_type=F32
        )

        def finish(hq, carry):
            for p in range(3):
                rows = pl.ds(pl.multiple_of(p * 256 + hq * 32, 32), 32)
                for e in range(2):
                    h = hq * 2 + e
                    residual = (base[h, p] - spread[rows, e * 128 : e * 128 + 128]).astype(BF16)
                    voltage = dot(residual, inv[h, p])
                    if w == ITERS - 1:
                        outv[h, p] = voltage
                    else:
                        rounded = voltage.astype(BF16)
                        vb[w + 1, h, p] = rounded
                        win[w + 1][1, h, p] = rounded
            return carry

        lax.fori_loop(0, 8, finish, 0, unroll=2)

    result = pltpu.make_async_copy(outv, out_hbm, out_sem)
    result.start()
    for w in range(ITERS):
        for copy in sweep_copies(w):
            copy.wait_send()
    result.wait()


def column_order():
    order = np.full((512,), -100000, np.int32)
    for pair in range(2):
        for slot in range(2):
            for h in range(16):
                for p in range(3):
                    for m in range(2):
                        order[pair * 256 + slot * 96 + h * 6 + p * 2 + m] = h * 6 + m * 3 + p
    return np.tile(order[None], (8, 1))


def per_device(n_bus, injection, inv_diag, off_tiles, pattern, coupling, site_map, bus_map):
    smem = pl.BlockSpec(memory_space=pltpu.SMEM)
    hbm = pl.BlockSpec(memory_space=pl.ANY)
    vmem = pl.BlockSpec(memory_space=pltpu.VMEM)
    dma = pltpu.SemaphoreType.DMA
    tiles = (16, 3, 32, 128)
    return pl.pallas_call(
        functools.partial(kernel, n_bus),
        out_shape=jax.ShapeDtypeStruct(tiles, F32),
        in_specs=[smem, smem, smem, vmem, hbm, hbm, hbm, hbm],
        out_specs=hbm,
        scratch_shapes=[
            pltpu.VMEM(tiles, BF16),
            pltpu.VMEM((16, 3, 128, 128), BF16),
            pltpu.VMEM((16, 3, 3, 128, 128), BF16),
            pltpu.VMEM((1536, 384), BF16),
            pltpu.VMEM((384, 512), BF16),
            pltpu.VMEM((1536, 512), BF16),
            pltpu.VMEM((ITERS,) + tiles, BF16),
            pltpu.VMEM((3,) + tiles, BF16),
            pltpu.VMEM((3,) + tiles, BF16),
            pltpu.VMEM((3, 32, 128), jnp.int32),
            pltpu.VMEM((96, 128), BF16),
            pltpu.VMEM((192, 256), BF16),
            pltpu.VMEM(tiles, F32),
            pltpu.VMEM((ITERS, 3, 32, 1536), BF16),
            pltpu.VMEM((ITERS, 2, 32, 1536), BF16),
            pltpu.VMEM((ITERS, 192, 512), BF16),
            pltpu.VMEM((ITERS, 192, 512), BF16),
            pltpu.VMEM((96, 512), F32),
            pltpu.VMEM((ITERS, 3, 64, 768), BF16),
            pltpu.VMEM((768, 256), F32),
            pltpu.VMEM(tiles, F32),
            dma((4,)),
            dma((ITERS * PER_SWEEP,)),
            dma((ITERS * PER_SWEEP,)),
            dma((2,)),
            dma((2,)),
            dma,
        ],
        compiler_params=pltpu.CompilerParams(
            collective_id=0, has_side_effects=True, vmem_limit_bytes=56 << 20
        ),
    )(
        site_map,
        bus_map,
        pattern,
        jnp.asarray(column_order()),
        injection,
        inv_diag,
        off_tiles,
        coupling.reshape(1536, 384),
    )


def solution(mesh):
    in_specs = (
        P("harm", "bus", None, None),
        P("harm", "bus", None, None),
        P("harm", "bus", None, None, None),
        P("bus", None),
        P("bus", None, "harm", None),
        P("bus"),
        P("bus"),
    )
    out_specs = P("harm", "bus", None, None)
    return jax.shard_map(
        functools.partial(per_device, mesh.shape["bus"]),
        mesh=mesh,
        in_specs=in_specs,
        out_specs=out_specs,
        check_vma=False,
    )
```

```python
import functools

import jax
import jax.numpy as jnp
import numpy as np
from jax import lax
from jax.experimental import pallas as pl
from jax.experimental.pallas import tpu as pltpu
from jax.sharding import PartitionSpec as P

ITERS = 2
MESH = pl.DeviceIdType.MESH
F32 = jnp.float32
BF16 = jnp.bfloat16

V_RUNS = ((0, 6), (6, 11), (11, 16))
T_RUNS = ((0, 64), (64, 96))
T_AFTER = (1, 2)


def dot(a, b):
    return jnp.dot(a, b, preferred_element_type=F32)


def block_swap(a, masks):
    out = a
    for k in range(1, 4):
        moved = pltpu.roll(pltpu.roll(a, 32 * k, 1), 8 - 2 * k, 0)
        out = jnp.where(masks[k], moved, out)
    return out


def kernel(
    n_bus,
    site_ref, bus_ref, pat_ref, order_ref, inj_hbm, inv_hbm, off_hbm, cpl_hbm,
    out_hbm,
    inj, inv, off, cpl, perm, bp, vb, win_0, win_1, tabs, ehot, hh, base, xs, tta, ttb, cur, zz, spread, resid,
    load_sem, v_send, v_recv, t_send, t_recv, f_send, f_recv, s_send, s_recv, z_send, z_recv, tab_send, tab_recv, out_sem,
):
    win = (win_0, win_1)
    me = lax.axis_index("bus")
    harm = lax.axis_index("harm")
    left = lax.rem(me + n_bus - 1, n_bus)
    right = lax.rem(me + 1, n_bus)
    zh, core = harm // 2, lax.rem(harm, 2)
    to_left, to_right = (left, harm), (right, harm)
    sibling = (me, zh * 2 + 1 - core)
    partner = (me, (1 - zh) * 2 + core)

    loads = [
        pltpu.make_async_copy(src, dst, load_sem.at[i])
        for i, (src, dst) in enumerate(((inj_hbm, inj), (inv_hbm, inv), (cpl_hbm, cpl), (off_hbm, off)))
    ]
    for load in loads:
        load.start()

    barrier = pltpu.get_barrier_semaphore()
    for peer in (to_left, to_right, sibling, partner):
        pl.semaphore_signal(barrier, inc=1, device_id=peer, device_id_type=MESH)

    def remote(src, dst, send, recv, peer):
        return pltpu.make_async_remote_copy(
            src_ref=src, dst_ref=dst, send_sem=send, recv_sem=recv, device_id=peer, device_id_type=MESH
        )

    tab_copies = [
        remote(tabs.at[1], tabs.at[0], tab_send.at[0], tab_recv.at[0], to_right),
        remote(tabs.at[1], tabs.at[2], tab_send.at[1], tab_recv.at[1], to_left),
    ]

    def v_copies(w, j):
        run = pl.ds(V_RUNS[j][0], V_RUNS[j][1] - V_RUNS[j][0])
        return [
            remote(vb.at[w, run], win[w].at[2, run], v_send.at[w, j, 0], v_recv.at[w, j, 0], to_left),
            remote(vb.at[w, run], win[w].at[0, run], v_send.at[w, j, 1], v_recv.at[w, j, 1], to_right),
        ]

    def rows_of(i, at):
        return pl.ds(at + T_RUNS[i][0], T_RUNS[i][1] - T_RUNS[i][0])

    def t_copy(w, i):
        return remote(
            tta.at[w, rows_of(i, 0)], ttb.at[w, rows_of(i, 0)], t_send.at[w, i], t_recv.at[w, i], partner
        )

    def f_copy(w, i):
        return remote(
            ttb.at[w, rows_of(i, 0)], ttb.at[w, rows_of(i, 96)], f_send.at[w, i], f_recv.at[w, i], sibling
        )

    def s_copy(w):
        return remote(tta.at[w, pl.ds(0, 96)], tta.at[w, pl.ds(96, 96)], s_send.at[w], s_recv.at[w], sibling)

    def z_copies(w):
        return [
            remote(zz.at[w, 1], zz.at[w, 2], z_send.at[w, 0], z_recv.at[w, 0], to_left),
            remote(zz.at[w, 1], zz.at[w, 0], z_send.at[w, 1], z_recv.at[w, 1], to_right),
        ]

    conv_row = lax.broadcasted_iota(jnp.int32, (32, 128), 0) // 2
    table = jnp.zeros((32, 128), jnp.int32)
    for c in range(16):
        table = jnp.where(conv_row == c, site_ref[c] * 128 + bus_ref[c], table)
    tabs[1] = table
    parity = lax.rem(lax.broadcasted_iota(jnp.int32, (32, 128), 0), 2)
    lane = lax.broadcasted_iota(jnp.int32, (32, 128), 1)
    for g in range(3):
        hit = (table + parity * 64) == (lane + (me - 1 + g) * 128)
        ehot[:, g * 128 : g * 128 + 128] = jnp.where(hit, 1.0, 0.0).astype(BF16)

    loads[0].wait()
    loads[1].wait()

    def first(h, carry):
        for p in range(3):
            rounded = dot(inj[h, p], inv[h, p]).astype(BF16)
            vb[0, h, p] = rounded
            win[0][1, h, p] = rounded
        return carry

    lax.fori_loop(0, 16, first, 0, unroll=4)

    pl.semaphore_wait(barrier, 4)
    for j in range(len(V_RUNS)):
        for copy in v_copies(0, j):
            copy.start()
    for copy in tab_copies:
        copy.start()

    sub = lax.broadcasted_iota(jnp.int32, (8, 128), 0) // 2
    chunk = lax.broadcasted_iota(jnp.int32, (8, 128), 1) // 32
    shift = lax.rem(chunk - sub + 4, 4)
    masks = [shift == k for k in range(4)]
    chunk96 = lax.broadcasted_iota(jnp.int32, (96, 128), 1) // 32
    chunk_masks = [chunk96 == k for k in range(4)]

    links = []
    for p in range(3):
        at = [pat_ref[p, k] - (me - 1) * 3 for k in range(3)]
        own = [(a >= 3) & (a < 6) for a in at]
        k0 = jnp.where(own[0], 0, jnp.where(own[1], 1, 2))
        k1 = jnp.where(k0 == 0, 1, 0)
        k2 = jnp.where(k0 == 2, 1, 2)

        def pick(k):
            return jnp.where(k == 0, at[0], jnp.where(k == 1, at[1], at[2]))

        links.append((k0, jnp.clip(pick(k0) - 3, 0, 2), k1, jnp.clip(pick(k1), 0, 8), k2, jnp.clip(pick(k2), 0, 8)))

    col = lax.broadcasted_iota(jnp.int32, (8, 512), 1)
    slot_bits = jnp.where(col < 256, jnp.where(col >= 96, 1, 0), jnp.where(col >= 384, 3, 2))
    source = jnp.bitwise_xor(slot_bits, harm) * 96 + order_ref[...]
    for r in range(48):
        row = lax.broadcasted_iota(jnp.int32, (8, 512), 0) + r * 8
        hot = jnp.where(row == source[0:1], 1.0, 0.0)
        if r % 2 == 0:
            kept = hot
        else:
            perm[(r - 1) * 8 : (r + 1) * 8] = jnp.concatenate([kept, hot], axis=0).astype(BF16)
    loads[2].wait()

    def permute(c, carry):
        rows = pl.ds(pl.multiple_of(c * 96, 96), 96)
        bp[rows] = dot(cpl[rows], perm[...]).astype(BF16)
        return carry

    lax.fori_loop(0, 16, permute, 0)
    loads[3].wait()

    for w in range(ITERS):

        def own_links(h, carry):
            for p in range(3):
                k0, own_at = links[p][:2]
                base[h, p] = inj[h, p].astype(F32) - dot(vb[w, h, own_at], off[h, p, k0])
            return carry

        lax.fori_loop(0, 16, own_links, 0, unroll=4)

        sent = 0
        for j, (start, stop) in enumerate(V_RUNS):
            for copy in v_copies(w, j):
                copy.wait_recv()
            count = (stop - start) * 96
            held = jnp.concatenate(
                [win[w][g, start:stop].reshape(count, 128) for g in range(3)], axis=1
            )
            xs[:, start * 96 : stop * 96] = lax.dot_general(
                ehot[...], held, (((1,), (1,)), ((), ())), preferred_element_type=F32
            )
            while sent < len(T_RUNS) and T_AFTER[sent] == j:
                for tp in range(T_RUNS[sent][0] // 16, T_RUNS[sent][1] // 16):
                    for u in range(4):
                        swapped = [
                            block_swap(xs[u * 8 : u * 8 + 8, t * 128 : t * 128 + 128], masks)
                            for t in (2 * tp, 2 * tp + 1)
                        ]
                        tta[w, tp * 16 : tp * 16 + 16, u * 128 : u * 128 + 128] = jnp.concatenate(
                            swapped, axis=0
                        ).astype(BF16)
                t_copy(w, sent).start()
                sent += 1
        s_copy(w).start()

        if w == 0:
            for copy in tab_copies:
                copy.wait()
            row256 = lax.rem(lax.broadcasted_iota(jnp.int32, (32, 256), 0), 2)
            lane256 = lax.broadcasted_iota(jnp.int32, (32, 256), 1)
            bus256 = lax.rem(lane256, 64) + me * 128
            part256 = lane256 // 64
            for g in range(3):
                wide = jnp.concatenate([tabs[g], tabs[g]], axis=1)
                for m in range(2):
                    hit = (wide == bus256) & (part256 == row256 * 2 + m)
                    at = g * 64 + m * 32
                    hh[at : at + 32] = jnp.where(hit, 1.0, 0.0).astype(BF16)

        def other_links(h, carry):
            for p in range(3):
                _, _, k1, at1, k2, at2 = links[p]
                columns = jnp.concatenate(
                    [win[w][at1 // 3, h, lax.rem(at1, 3)], win[w][at2 // 3, h, lax.rem(at2, 3)]], axis=1
                )
                tiles = jnp.concatenate([off[h, p, k1], off[h, p, k2]], axis=0)
                base[h, p] = base[h, p] - dot(columns, tiles)
            return carry

        lax.fori_loop(0, 16, other_links, 0, unroll=4)

        def couple(held, top, rows, at, add):
            for u in range(4):
                rhs = held[w, top : top + rows, u * 128 : u * 128 + 128]
                total = None
                for q in range(4):
                    c = u * 4 + q
                    one = dot(bp[c * 96 : c * 96 + 96, at : at + rows], rhs)
                    total = one if total is None else jnp.where(chunk_masks[q], one, total)
                lanes = slice(u * 128, u * 128 + 128)
                cur[:, lanes] = cur[:, lanes] + total if add else total

        s_copy(w).wait_recv()
        couple(tta, 0, 192, 0, False)
        for i in range(len(T_RUNS)):
            t_copy(w, i).wait_recv()
            f_copy(w, i).start()
        couple(ttb, 0, 96, 256, True)
        for i in range(len(T_RUNS)):
            f_copy(w, i).wait_recv()
        couple(ttb, 96, 96, 384, True)

        for up in range(2):
            for j in range(12):
                m, ph = j // 6, j % 6
                swapped = [
                    block_swap(cur[j * 8 : j * 8 + 8, u * 128 : u * 128 + 128], masks)
                    for u in (2 * up, 2 * up + 1)
                ]
                at = m * 32 + up * 16
                zz[w, 1, at : at + 16, ph * 128 : ph * 128 + 128] = jnp.concatenate(
                    swapped, axis=0
                ).astype(BF16)
        for copy in z_copies(w):
            copy.start()
        for copy in z_copies(w):
            copy.wait_recv()
        spread[...] = lax.dot_general(
            zz[w].reshape(192, 768), hh[...], (((0,), (0,)), ((), ())), preferred_element_type=F32
        )

        def finish(h, carry):
            hq, e = h // 2, lax.rem(h, 2)
            for p in range(3):
                rows = pl.ds(pl.multiple_of(p * 256 + hq * 32, 32), 32)
                lanes = pl.ds(pl.multiple_of(e * 128, 128), 128)
                residual = (base[h, p] - spread[rows, lanes]).astype(BF16)
                if w == ITERS - 1:
                    resid[h, p] = residual
                else:
                    rounded = dot(residual, inv[h, p]).astype(BF16)
                    vb[w + 1, h, p] = rounded
                    win[w + 1][1, h, p] = rounded
            return carry

        if w < ITERS - 1:
            for j, (start, stop) in enumerate(V_RUNS):
                lax.fori_loop(start, stop, finish, 0, unroll=stop - start)
                for copy in v_copies(w + 1, j):
                    copy.start()
        else:
            lax.fori_loop(0, 16, finish, 0, unroll=4)

    result = pltpu.make_async_copy(resid, out_hbm, out_sem)
    result.start()
    for w in range(ITERS):
        for j in range(len(V_RUNS)):
            for copy in v_copies(w, j):
                copy.wait_send()
        for i in range(len(T_RUNS)):
            t_copy(w, i).wait_send()
            f_copy(w, i).wait_send()
        s_copy(w).wait_send()
        for copy in z_copies(w):
            copy.wait_send()
    result.wait()


def column_order():
    order = np.full((512,), -100000, np.int32)
    for start in (0, 96, 256, 384):
        for h in range(16):
            for p in range(3):
                for m in range(2):
                    order[start + h * 6 + p * 2 + m] = h * 6 + m * 3 + p
    return np.tile(order[None], (8, 1))


def per_device(n_bus, injection, inv_diag, off_tiles, pattern, coupling, site_map, bus_map):
    smem = pl.BlockSpec(memory_space=pltpu.SMEM)
    hbm = pl.BlockSpec(memory_space=pl.ANY)
    vmem = pl.BlockSpec(memory_space=pltpu.VMEM)
    dma = pltpu.SemaphoreType.DMA
    tiles = (16, 3, 32, 128)
    runs, parts = len(V_RUNS), len(T_RUNS)
    residual = pl.pallas_call(
        functools.partial(kernel, n_bus),
        out_shape=jax.ShapeDtypeStruct(tiles, BF16),
        in_specs=[smem, smem, smem, vmem, hbm, hbm, hbm, hbm],
        out_specs=hbm,
        scratch_shapes=[
            pltpu.VMEM(tiles, BF16),
            pltpu.VMEM((16, 3, 128, 128), BF16),
            pltpu.VMEM((16, 3, 3, 128, 128), BF16),
            pltpu.VMEM((1536, 384), BF16),
            pltpu.VMEM((384, 512), BF16),
            pltpu.VMEM((1536, 512), BF16),
            pltpu.VMEM((ITERS,) + tiles, BF16),
            pltpu.VMEM((3,) + tiles, BF16),
            pltpu.VMEM((3,) + tiles, BF16),
            pltpu.VMEM((3, 32, 128), jnp.int32),
            pltpu.VMEM((32, 384), BF16),
            pltpu.VMEM((192, 256), BF16),
            pltpu.VMEM(tiles, F32),
            pltpu.VMEM((32, 1536), F32),
            pltpu.VMEM((ITERS, 192, 512), BF16),
            pltpu.VMEM((ITERS, 192, 512), BF16),
            pltpu.VMEM((96, 512), F32),
            pltpu.VMEM((ITERS, 3, 64, 768), BF16),
            pltpu.VMEM((768, 256), F32),
            pltpu.VMEM(tiles, BF16),
            dma((4,)),
            dma((ITERS, runs, 2)),
            dma((ITERS, runs, 2)),
            dma((ITERS, parts)),
            dma((ITERS, parts)),
            dma((ITERS, parts)),
            dma((ITERS, parts)),
            dma((ITERS,)),
            dma((ITERS,)),
            dma((ITERS, 2)),
            dma((ITERS, 2)),
            dma((2,)),
            dma((2,)),
            dma,
        ],
        compiler_params=pltpu.CompilerParams(
            collective_id=0, has_side_effects=True, vmem_limit_bytes=56 << 20
        ),
    )(
        site_map,
        bus_map,
        pattern,
        jnp.asarray(column_order()),
        injection,
        inv_diag,
        off_tiles,
        coupling.reshape(1536, 384),
    )
    return jnp.einsum("htsa,htab->htsb", residual, inv_diag, preferred_element_type=F32)


def solution(mesh):
    in_specs = (
        P("harm", "bus", None, None),
        P("harm", "bus", None, None),
        P("harm", "bus", None, None, None),
        P("bus", None),
        P("bus", None, "harm", None),
        P("bus"),
        P("bus"),
    )
    out_specs = P("harm", "bus", None, None)
    return jax.shard_map(
        functools.partial(per_device, mesh.shape["bus"]),
        mesh=mesh,
        in_specs=in_specs,
        out_specs=out_specs,
        check_vma=False,
    )
```

```python
import functools

import jax
import jax.numpy as jnp
import numpy as np
from jax import lax
from jax.experimental import pallas as pl
from jax.experimental.pallas import tpu as pltpu
from jax.sharding import PartitionSpec as P

ITERS = 2
MESH = pl.DeviceIdType.MESH
F32 = jnp.float32
BF16 = jnp.bfloat16

V_RUNS = ((0, 8), (8, 16))
HALF_ROWS = 48
DIRECT = ()


def dot(a, b):
    return jnp.dot(a, b, preferred_element_type=F32)


def block_swap(a, masks):
    out = a
    for k in range(1, 4):
        moved = pltpu.roll(pltpu.roll(a, 32 * k, 1), 8 - 2 * k, 0)
        out = jnp.where(masks[k], moved, out)
    return out


def kernel(
    n_bus,
    site_ref, bus_ref, pat_ref, order_ref, inj_hbm, inv_hbm, off_hbm, cpl_hbm,
    out_hbm,
    inj, inv, off, cpl, perm, bp, vb, win_0, win_1, tabs, ehot, hh, base, xs, xr, tta, ttb, cur, zz, spread, resid,
    load_sem, v_send, v_recv, x_send, x_recv, t_send, t_recv, f_send, f_recv, s_send, s_recv, z_send, z_recv, tab_send, tab_recv, out_sem,
):
    win = (win_0, win_1)
    me = lax.axis_index("bus")
    harm = lax.axis_index("harm")
    left = lax.rem(me + n_bus - 1, n_bus)
    right = lax.rem(me + 1, n_bus)
    zh, core = harm // 2, lax.rem(harm, 2)
    to_left, to_right = (left, harm), (right, harm)
    sibling = (me, zh * 2 + 1 - core)
    partner = (me, (1 - zh) * 2 + core)
    across = (me, (1 - zh) * 2 + 1 - core)

    loads = [
        pltpu.make_async_copy(src, dst, load_sem.at[i])
        for i, (src, dst) in enumerate(((inj_hbm, inj), (inv_hbm, inv), (cpl_hbm, cpl), (off_hbm, off)))
    ]
    for load in loads:
        load.start()

    barrier = pltpu.get_barrier_semaphore()
    for peer in (to_left, to_right, sibling, partner, across):
        pl.semaphore_signal(barrier, inc=1, device_id=peer, device_id_type=MESH)

    def remote(src, dst, send, recv, peer):
        return pltpu.make_async_remote_copy(
            src_ref=src, dst_ref=dst, send_sem=send, recv_sem=recv, device_id=peer, device_id_type=MESH
        )

    tab_copies = [
        remote(tabs.at[1], tabs.at[0], tab_send.at[0], tab_recv.at[0], to_right),
        remote(tabs.at[1], tabs.at[2], tab_send.at[1], tab_recv.at[1], to_left),
    ]

    def v_copies(w, j):
        run = pl.ds(V_RUNS[j][0], V_RUNS[j][1] - V_RUNS[j][0])
        return [
            remote(vb.at[w, run], win[w].at[2, run], v_send.at[w, j, 0], v_recv.at[w, j, 0], to_left),
            remote(vb.at[w, run], win[w].at[0, run], v_send.at[w, j, 1], v_recv.at[w, j, 1], to_right),
        ]

    def x_copies(w, j):
        lanes = pl.ds(j * 768, 768)
        return [
            remote(xs.at[w, 0, :, lanes], xr.at[w, 1, :, lanes], x_send.at[w, j, 0], x_recv.at[w, j, 0], to_left),
            remote(xs.at[w, 2, :, lanes], xr.at[w, 0, :, lanes], x_send.at[w, j, 1], x_recv.at[w, j, 1], to_right),
        ]

    def rows_of(j, at):
        return pl.ds(at + j * HALF_ROWS, HALF_ROWS)

    def t_copy(w, j):
        return remote(
            tta.at[w, rows_of(j, 0)], ttb.at[w, rows_of(j, 0)], t_send.at[w, j], t_recv.at[w, j], partner
        )

    def f_copy(w, j):
        if j in DIRECT:
            return remote(
                tta.at[w, rows_of(j, 0)], ttb.at[w, rows_of(j, 96)], f_send.at[w, j], f_recv.at[w, j], across
            )
        return remote(
            ttb.at[w, rows_of(j, 0)], ttb.at[w, rows_of(j, 96)], f_send.at[w, j], f_recv.at[w, j], sibling
        )

    def s_copy(w):
        return remote(tta.at[w, pl.ds(0, 96)], tta.at[w, pl.ds(96, 96)], s_send.at[w], s_recv.at[w], sibling)

    def z_copies(w, up):
        rows = pl.ds(up * 32, 32)
        return [
            remote(zz.at[w, 1, rows], zz.at[w, 2, rows], z_send.at[w, up, 0], z_recv.at[w, up, 0], to_left),
            remote(zz.at[w, 1, rows], zz.at[w, 0, rows], z_send.at[w, up, 1], z_recv.at[w, up, 1], to_right),
        ]

    conv_row = lax.broadcasted_iota(jnp.int32, (32, 128), 0) // 2
    table = jnp.zeros((32, 128), jnp.int32)
    for c in range(16):
        table = jnp.where(conv_row == c, site_ref[c] * 128 + bus_ref[c], table)
    tabs[1] = table

    loads[0].wait()
    loads[1].wait()

    def first(h, carry):
        for p in range(3):
            rounded = dot(inj[h, p], inv[h, p]).astype(BF16)
            vb[0, h, p] = rounded
            win[0][1, h, p] = rounded
        return carry

    lax.fori_loop(0, 16, first, 0, unroll=4)

    pl.semaphore_wait(barrier, 5)
    for copy in tab_copies + v_copies(0, 0):
        copy.start()

    sub = lax.broadcasted_iota(jnp.int32, (8, 128), 0) // 2
    chunk = lax.broadcasted_iota(jnp.int32, (8, 128), 1) // 32
    shift = lax.rem(chunk - sub + 4, 4)
    masks = [shift == k for k in range(4)]
    chunk96 = lax.broadcasted_iota(jnp.int32, (96, 128), 1) // 32
    chunk_masks = [chunk96 == k for k in range(4)]

    links = []
    for p in range(3):
        at = [pat_ref[p, k] - (me - 1) * 3 for k in range(3)]
        own = [(a >= 3) & (a < 6) for a in at]
        k0 = jnp.where(own[0], 0, jnp.where(own[1], 1, 2))
        k1 = jnp.where(k0 == 0, 1, 0)
        k2 = jnp.where(k0 == 2, 1, 2)

        def pick(k):
            return jnp.where(k == 0, at[0], jnp.where(k == 1, at[1], at[2]))

        links.append((k0, jnp.clip(pick(k0) - 3, 0, 2), k1, jnp.clip(pick(k1), 0, 8), k2, jnp.clip(pick(k2), 0, 8)))

    def pick_half(w, j):
        for part in range(3):
            held = vb[w, j * 8 : j * 8 + 8].reshape(768, 128)[part * 256 : part * 256 + 256]
            got = lax.dot_general(
                ehot[...], held, (((1,), (1,)), ((), ())), preferred_element_type=F32
            ).astype(BF16)
            at = j * 768 + part * 256
            for g in range(3):
                xs[w, g, :, at : at + 256] = got[g * 32 : g * 32 + 32]
        for copy in x_copies(w, j):
            copy.start()

    for copy in tab_copies:
        copy.wait()
    parity = lax.rem(lax.broadcasted_iota(jnp.int32, (32, 128), 0), 2)
    lane = lax.broadcasted_iota(jnp.int32, (32, 128), 1)
    for g in range(3):
        hit = (tabs[g] + parity * 64) == (lane + me * 128)
        ehot[g * 32 : g * 32 + 32] = jnp.where(hit, 1.0, 0.0).astype(BF16)
    for j in range(2):
        pick_half(0, j)

    row256 = lax.rem(lax.broadcasted_iota(jnp.int32, (16, 256), 0), 2)
    lane256 = lax.broadcasted_iota(jnp.int32, (16, 256), 1)
    bus256 = lax.rem(lane256, 64) + me * 128
    part256 = lane256 // 64
    for g in range(3):
        for up in range(2):
            tab = tabs[g, up * 16 : up * 16 + 16]
            wide = jnp.concatenate([tab, tab], axis=1)
            for m in range(2):
                hit = (wide == bus256) & (part256 == row256 * 2 + m)
                at = g * 64 + up * 32 + m * 16
                hh[at : at + 16] = jnp.where(hit, 1.0, 0.0).astype(BF16)

    col = lax.broadcasted_iota(jnp.int32, (8, 512), 1)
    slot_bits = jnp.where(col < 256, jnp.where(col >= 96, 1, 0), jnp.where(col >= 384, 3, 2))
    source = jnp.bitwise_xor(slot_bits, harm) * 96 + order_ref[...]
    for r in range(48):
        row = lax.broadcasted_iota(jnp.int32, (8, 512), 0) + r * 8
        hot = jnp.where(row == source[0:1], 1.0, 0.0)
        if r % 2 == 0:
            kept = hot
        else:
            perm[(r - 1) * 8 : (r + 1) * 8] = jnp.concatenate([kept, hot], axis=0).astype(BF16)
    loads[2].wait()

    def permute(c, carry):
        rows = pl.ds(pl.multiple_of(c * 96, 96), 96)
        bp[rows] = dot(cpl[rows], perm[...]).astype(BF16)
        return carry

    lax.fori_loop(0, 16, permute, 0)
    loads[3].wait()

    for w in range(ITERS):

        def own_links(h, carry):
            for p in range(3):
                k0, own_at = links[p][:2]
                base[h, p] = inj[h, p].astype(F32) - dot(vb[w, h, own_at], off[h, p, k0])
            return carry

        lax.fori_loop(0, 16, own_links, 0, unroll=4)

        for j in range(2):
            for copy in x_copies(w, j):
                copy.wait_recv()
            for tp in range(3 * j, 3 * j + 3):
                for up in range(2):
                    both = []
                    for t in (2 * tp, 2 * tp + 1):
                        rows, lanes = slice(up * 16, up * 16 + 16), slice(t * 128, t * 128 + 128)
                        both.append(
                            xs[w, 1, rows, lanes].astype(F32)
                            + xr[w, 0, rows, lanes].astype(F32)
                            + xr[w, 1, rows, lanes].astype(F32)
                        )
                    for half in range(2):
                        u = up * 2 + half
                        swapped = [block_swap(b[half * 8 : half * 8 + 8], masks) for b in both]
                        tta[w, tp * 16 : tp * 16 + 16, u * 128 : u * 128 + 128] = jnp.concatenate(
                            swapped, axis=0
                        ).astype(BF16)
            t_copy(w, j).start()
            if j in DIRECT:
                f_copy(w, j).start()
        s_copy(w).start()

        def couple(held, top, rows, at, add, tiles=range(4)):
            for u in tiles:
                rhs = held[w, top : top + rows, u * 128 : u * 128 + 128]
                total = None
                for q in range(4):
                    c = u * 4 + q
                    one = dot(bp[c * 96 : c * 96 + 96, at : at + rows], rhs)
                    total = one if total is None else jnp.where(chunk_masks[q], one, total)
                lanes = slice(u * 128, u * 128 + 128)
                cur[:, lanes] = cur[:, lanes] + total if add else total

        for j in range(2):
            t_copy(w, j).wait_send()
            if j in DIRECT:
                f_copy(w, j).wait_send()
        for copy in v_copies(w, 1):
            copy.start()
        s_copy(w).wait_recv()
        couple(tta, 0, 192, 0, False)
        for j in range(2):
            t_copy(w, j).wait_recv()
            if j not in DIRECT:
                f_copy(w, j).start()
        couple(ttb, 0, 96, 256, True)
        for j in range(2):
            f_copy(w, j).wait_recv()

        for up in range(2):
            couple(ttb, 96, 96, 384, True, (2 * up, 2 * up + 1))
            for j in range(12):
                m, ph = j // 6, j % 6
                swapped = [
                    block_swap(cur[j * 8 : j * 8 + 8, u * 128 : u * 128 + 128], masks)
                    for u in (2 * up, 2 * up + 1)
                ]
                at = up * 32 + m * 16
                zz[w, 1, at : at + 16, ph * 128 : ph * 128 + 128] = jnp.concatenate(
                    swapped, axis=0
                ).astype(BF16)
            for copy in z_copies(w, up):
                copy.start()

        for j in range(2):
            for copy in v_copies(w, j):
                copy.wait_recv()

        def other_links(h, carry):
            for p in range(3):
                _, _, k1, at1, k2, at2 = links[p]
                columns = jnp.concatenate(
                    [win[w][at1 // 3, h, lax.rem(at1, 3)], win[w][at2 // 3, h, lax.rem(at2, 3)]], axis=1
                )
                tiles = jnp.concatenate([off[h, p, k1], off[h, p, k2]], axis=0)
                base[h, p] = base[h, p] - dot(columns, tiles)
            return carry

        lax.fori_loop(0, 16, other_links, 0, unroll=4)

        for up in range(2):
            for copy in z_copies(w, up):
                copy.wait_recv()
        spread[...] = lax.dot_general(
            zz[w].reshape(192, 768), hh[...], (((0,), (0,)), ((), ())), preferred_element_type=F32
        )

        def finish(h, carry):
            hq, e = h // 2, lax.rem(h, 2)
            for p in range(3):
                rows = pl.ds(pl.multiple_of(p * 256 + hq * 32, 32), 32)
                lanes = pl.ds(pl.multiple_of(e * 128, 128), 128)
                residual = (base[h, p] - spread[rows, lanes]).astype(BF16)
                if w == ITERS - 1:
                    resid[h, p] = residual
                else:
                    rounded = dot(residual, inv[h, p]).astype(BF16)
                    vb[w + 1, h, p] = rounded
                    win[w + 1][1, h, p] = rounded
            return carry

        if w < ITERS - 1:
            for j in range(2):
                lax.fori_loop(j * 8, j * 8 + 8, finish, 0, unroll=4)
                pick_half(w + 1, j)
            for copy in v_copies(w + 1, 0):
                copy.start()
        else:
            lax.fori_loop(0, 16, finish, 0, unroll=4)

    result = pltpu.make_async_copy(resid, out_hbm, out_sem)
    result.start()
    for w in range(ITERS):
        for j in range(2):
            for copy in v_copies(w, j) + x_copies(w, j) + z_copies(w, j):
                copy.wait_send()
            if j not in DIRECT:
                f_copy(w, j).wait_send()
        s_copy(w).wait_send()
    result.wait()


def column_order():
    order = np.full((512,), -100000, np.int32)
    for start in (0, 96, 256, 384):
        for h in range(16):
            for p in range(3):
                for m in range(2):
                    order[start + h * 6 + p * 2 + m] = h * 6 + m * 3 + p
    return np.tile(order[None], (8, 1))


def per_device(n_bus, injection, inv_diag, off_tiles, pattern, coupling, site_map, bus_map):
    smem = pl.BlockSpec(memory_space=pltpu.SMEM)
    hbm = pl.BlockSpec(memory_space=pl.ANY)
    vmem = pl.BlockSpec(memory_space=pltpu.VMEM)
    dma = pltpu.SemaphoreType.DMA
    tiles = (16, 3, 32, 128)
    residual = pl.pallas_call(
        functools.partial(kernel, n_bus),
        out_shape=jax.ShapeDtypeStruct(tiles, BF16),
        in_specs=[smem, smem, smem, vmem, hbm, hbm, hbm, hbm],
        out_specs=hbm,
        scratch_shapes=[
            pltpu.VMEM(tiles, BF16),
            pltpu.VMEM((16, 3, 128, 128), BF16),
            pltpu.VMEM((16, 3, 3, 128, 128), BF16),
            pltpu.VMEM((1536, 384), BF16),
            pltpu.VMEM((384, 512), BF16),
            pltpu.VMEM((1536, 512), BF16),
            pltpu.VMEM((ITERS,) + tiles, BF16),
            pltpu.VMEM((3,) + tiles, BF16),
            pltpu.VMEM((3,) + tiles, BF16),
            pltpu.VMEM((3, 32, 128), jnp.int32),
            pltpu.VMEM((96, 128), BF16),
            pltpu.VMEM((192, 256), BF16),
            pltpu.VMEM(tiles, F32),
            pltpu.VMEM((ITERS, 3, 32, 1536), BF16),
            pltpu.VMEM((ITERS, 2, 32, 1536), BF16),
            pltpu.VMEM((ITERS, 192, 512), BF16),
            pltpu.VMEM((ITERS, 192, 512), BF16),
            pltpu.VMEM((96, 512), F32),
            pltpu.VMEM((ITERS, 3, 64, 768), BF16),
            pltpu.VMEM((768, 256), F32),
            pltpu.VMEM(tiles, BF16),
            dma((4,)),
            dma((ITERS, 2, 2)),
            dma((ITERS, 2, 2)),
            dma((ITERS, 2, 2)),
            dma((ITERS, 2, 2)),
            dma((ITERS, 2)),
            dma((ITERS, 2)),
            dma((ITERS, 2)),
            dma((ITERS, 2)),
            dma((ITERS,)),
            dma((ITERS,)),
            dma((ITERS, 2, 2)),
            dma((ITERS, 2, 2)),
            dma((2,)),
            dma((2,)),
            dma,
        ],
        compiler_params=pltpu.CompilerParams(
            collective_id=0, has_side_effects=True, vmem_limit_bytes=56 << 20
        ),
    )(
        site_map,
        bus_map,
        pattern,
        jnp.asarray(column_order()),
        injection,
        inv_diag,
        off_tiles,
        coupling.reshape(1536, 384),
    )
    return jnp.einsum("htsa,htab->htsb", residual, inv_diag, preferred_element_type=F32)


def solution(mesh):
    in_specs = (
        P("harm", "bus", None, None),
        P("harm", "bus", None, None),
        P("harm", "bus", None, None, None),
        P("bus", None),
        P("bus", None, "harm", None),
        P("bus"),
        P("bus"),
    )
    out_specs = P("harm", "bus", None, None)
    return jax.shard_map(
        functools.partial(per_device, mesh.shape["bus"]),
        mesh=mesh,
        in_specs=in_specs,
        out_specs=out_specs,
        check_vma=False,
    )
```

```python
import functools

import jax
import jax.numpy as jnp
import numpy as np
from jax import lax
from jax.experimental import pallas as pl
from jax.experimental.pallas import tpu as pltpu
from jax.sharding import PartitionSpec as P

ITERS = 2
MESH = pl.DeviceIdType.MESH
F32 = jnp.float32
BF16 = jnp.bfloat16

V_RUNS = ((0, 8), (8, 16))
HALF_ROWS = 48


def dot(a, b):
    return jnp.dot(a, b, preferred_element_type=F32)


def block_swap(a, masks):
    out = a
    for k in range(1, 4):
        moved = pltpu.roll(pltpu.roll(a, 32 * k, 1), 8 - 2 * k, 0)
        out = jnp.where(masks[k], moved, out)
    return out


def kernel(
    n_bus,
    site_ref, bus_ref, pat_ref, order_ref, inj_hbm, inv_hbm, off_hbm, cpl_hbm,
    out_hbm,
    inj, inv, off, cpl, perm, bp, vb, win_0, win_1, tabs, ehot, wide_hot, hh, base, picked, xs, xr, tta, ttb, cur, zz, spread, resid,
    load_sem, v_send, v_recv, x_send, x_recv, t_send, t_recv, f_send, f_recv, s_send, s_recv, z_send, z_recv, tab_send, tab_recv, out_sem,
):
    win = (win_0, win_1)
    me = lax.axis_index("bus")
    harm = lax.axis_index("harm")
    left = lax.rem(me + n_bus - 1, n_bus)
    right = lax.rem(me + 1, n_bus)
    zh, core = harm // 2, lax.rem(harm, 2)
    to_left, to_right = (left, harm), (right, harm)
    sibling = (me, zh * 2 + 1 - core)
    partner = (me, (1 - zh) * 2 + core)

    loads = [
        pltpu.make_async_copy(src, dst, load_sem.at[i])
        for i, (src, dst) in enumerate(((inj_hbm, inj), (inv_hbm, inv), (cpl_hbm, cpl), (off_hbm, off)))
    ]
    for load in loads:
        load.start()

    barrier = pltpu.get_barrier_semaphore()
    for peer in (to_left, to_right, sibling, partner):
        pl.semaphore_signal(barrier, inc=1, device_id=peer, device_id_type=MESH)

    def remote(src, dst, send, recv, peer):
        return pltpu.make_async_remote_copy(
            src_ref=src, dst_ref=dst, send_sem=send, recv_sem=recv, device_id=peer, device_id_type=MESH
        )

    tab_copies = [
        remote(tabs.at[1], tabs.at[0], tab_send.at[0], tab_recv.at[0], to_right),
        remote(tabs.at[1], tabs.at[2], tab_send.at[1], tab_recv.at[1], to_left),
    ]

    def v_copies(w, j):
        run = pl.ds(V_RUNS[j][0], V_RUNS[j][1] - V_RUNS[j][0])
        return [
            remote(vb.at[w, run], win[w].at[2, run], v_send.at[w, j, 0], v_recv.at[w, j, 0], to_left),
            remote(vb.at[w, run], win[w].at[0, run], v_send.at[w, j, 1], v_recv.at[w, j, 1], to_right),
        ]

    def x_copies(w, j):
        lanes = pl.ds(j * 768, 768)
        return [
            remote(xs.at[w, 0, :, lanes], xr.at[w, 1, :, lanes], x_send.at[w, j, 0], x_recv.at[w, j, 0], to_left),
            remote(xs.at[w, 2, :, lanes], xr.at[w, 0, :, lanes], x_send.at[w, j, 1], x_recv.at[w, j, 1], to_right),
        ]

    def rows_of(j, at):
        return pl.ds(at + j * HALF_ROWS, HALF_ROWS)

    def t_copy(w, j):
        return remote(
            tta.at[w, rows_of(j, 0)], ttb.at[w, rows_of(j, 0)], t_send.at[w, j], t_recv.at[w, j], partner
        )

    def f_copy(w, j):
        return remote(
            ttb.at[w, rows_of(j, 0)], ttb.at[w, rows_of(j, 96)], f_send.at[w, j], f_recv.at[w, j], sibling
        )

    def s_copy(w):
        return remote(tta.at[w, pl.ds(0, 96)], tta.at[w, pl.ds(96, 96)], s_send.at[w], s_recv.at[w], sibling)

    def z_copies(w, up):
        rows = pl.ds(up * 32, 32)
        return [
            remote(zz.at[w, 1, rows], zz.at[w, 2, rows], z_send.at[w, up, 0], z_recv.at[w, up, 0], to_left),
            remote(zz.at[w, 1, rows], zz.at[w, 0, rows], z_send.at[w, up, 1], z_recv.at[w, up, 1], to_right),
        ]

    conv_row = lax.broadcasted_iota(jnp.int32, (32, 128), 0) // 2
    table = jnp.zeros((32, 128), jnp.int32)
    for c in range(16):
        table = jnp.where(conv_row == c, site_ref[c] * 128 + bus_ref[c], table)
    tabs[1] = table
    parity = lax.rem(lax.broadcasted_iota(jnp.int32, (32, 128), 0), 2)
    lane = lax.broadcasted_iota(jnp.int32, (32, 128), 1)
    for g in range(3):
        hit = (table + parity * 64) == (lane + (me - 1 + g) * 128)
        wide_hot[:, g * 128 : g * 128 + 128] = jnp.where(hit, 1.0, 0.0).astype(BF16)

    loads[0].wait()
    loads[1].wait()

    def first(h, carry):
        for p in range(3):
            rounded = dot(inj[h, p], inv[h, p]).astype(BF16)
            vb[0, h, p] = rounded
            win[0][1, h, p] = rounded
        return carry

    lax.fori_loop(0, 16, first, 0, unroll=4)

    pl.semaphore_wait(barrier, 4)
    for copy in tab_copies + v_copies(0, 0):
        copy.start()

    sub = lax.broadcasted_iota(jnp.int32, (8, 128), 0) // 2
    chunk = lax.broadcasted_iota(jnp.int32, (8, 128), 1) // 32
    shift = lax.rem(chunk - sub + 4, 4)
    masks = [shift == k for k in range(4)]
    chunk96 = lax.broadcasted_iota(jnp.int32, (96, 128), 1) // 32
    chunk_masks = [chunk96 == k for k in range(4)]

    links = []
    for p in range(3):
        at = [pat_ref[p, k] - (me - 1) * 3 for k in range(3)]
        own = [(a >= 3) & (a < 6) for a in at]
        k0 = jnp.where(own[0], 0, jnp.where(own[1], 1, 2))
        k1 = jnp.where(k0 == 0, 1, 0)
        k2 = jnp.where(k0 == 2, 1, 2)

        def pick(k):
            return jnp.where(k == 0, at[0], jnp.where(k == 1, at[1], at[2]))

        links.append((k0, jnp.clip(pick(k0) - 3, 0, 2), k1, jnp.clip(pick(k1), 0, 8), k2, jnp.clip(pick(k2), 0, 8)))

    def pick_half(w, j):
        for part in range(3):
            held = vb[w, j * 8 : j * 8 + 8].reshape(768, 128)[part * 256 : part * 256 + 256]
            got = lax.dot_general(
                ehot[...], held, (((1,), (1,)), ((), ())), preferred_element_type=F32
            ).astype(BF16)
            at = j * 768 + part * 256
            for g in range(3):
                xs[w, g, :, at : at + 256] = got[g * 32 : g * 32 + 32]
        for copy in x_copies(w, j):
            copy.start()

    for copy in tab_copies:
        copy.wait()
    for g in range(3):
        hit = (tabs[g] + parity * 64) == (lane + me * 128)
        ehot[g * 32 : g * 32 + 32] = jnp.where(hit, 1.0, 0.0).astype(BF16)
    pick_half(0, 1)

    row256 = lax.rem(lax.broadcasted_iota(jnp.int32, (16, 256), 0), 2)
    lane256 = lax.broadcasted_iota(jnp.int32, (16, 256), 1)
    bus256 = lax.rem(lane256, 64) + me * 128
    part256 = lane256 // 64
    for g in range(3):
        for up in range(2):
            tab = tabs[g, up * 16 : up * 16 + 16]
            wide = jnp.concatenate([tab, tab], axis=1)
            for m in range(2):
                hit = (wide == bus256) & (part256 == row256 * 2 + m)
                at = g * 64 + up * 32 + m * 16
                hh[at : at + 16] = jnp.where(hit, 1.0, 0.0).astype(BF16)

    col = lax.broadcasted_iota(jnp.int32, (8, 512), 1)
    slot_bits = jnp.where(col < 256, jnp.where(col >= 96, 1, 0), jnp.where(col >= 384, 3, 2))
    source = jnp.bitwise_xor(slot_bits, harm) * 96 + order_ref[...]
    for r in range(48):
        row = lax.broadcasted_iota(jnp.int32, (8, 512), 0) + r * 8
        hot = jnp.where(row == source[0:1], 1.0, 0.0)
        if r % 2 == 0:
            kept = hot
        else:
            perm[(r - 1) * 8 : (r + 1) * 8] = jnp.concatenate([kept, hot], axis=0).astype(BF16)
    loads[2].wait()

    def permute(c, carry):
        rows = pl.ds(pl.multiple_of(c * 96, 96), 96)
        bp[rows] = dot(cpl[rows], perm[...]).astype(BF16)
        return carry

    lax.fori_loop(0, 16, permute, 0)
    loads[3].wait()

    results = []
    for j in range(2):
        half = pl.ds(j * 8, 8)
        results.append(pltpu.make_async_copy(resid.at[half], out_hbm.at[half], out_sem.at[j]))

    for w in range(ITERS):

        def own_links(h, carry):
            for p in range(3):
                k0, own_at = links[p][:2]
                base[h, p] = inj[h, p].astype(F32) - dot(vb[w, h, own_at], off[h, p, k0])
            return carry

        lax.fori_loop(0, 16, own_links, 0, unroll=4)

        for j in range(2):
            if (w, j) == (0, 0):
                for copy in v_copies(0, 0):
                    copy.wait_recv()
                for part in range(3):
                    held = jnp.concatenate(
                        [
                            win[0][g, 0:8].reshape(768, 128)[part * 256 : part * 256 + 256]
                            for g in range(3)
                        ],
                        axis=1,
                    )
                    picked[:, part * 256 : part * 256 + 256] = lax.dot_general(
                        wide_hot[...], held, (((1,), (1,)), ((), ())), preferred_element_type=F32
                    )
            else:
                for copy in x_copies(w, j):
                    copy.wait_recv()
            for tp in range(3 * j, 3 * j + 3):
                for up in range(2):
                    both = []
                    for t in (2 * tp, 2 * tp + 1):
                        rows, lanes = slice(up * 16, up * 16 + 16), slice(t * 128, t * 128 + 128)
                        if (w, j) == (0, 0):
                            both.append(picked[rows, lanes])
                            continue
                        both.append(
                            xs[w, 1, rows, lanes].astype(F32)
                            + xr[w, 0, rows, lanes].astype(F32)
                            + xr[w, 1, rows, lanes].astype(F32)
                        )
                    for half in range(2):
                        u = up * 2 + half
                        swapped = [block_swap(b[half * 8 : half * 8 + 8], masks) for b in both]
                        tta[w, tp * 16 : tp * 16 + 16, u * 128 : u * 128 + 128] = jnp.concatenate(
                            swapped, axis=0
                        ).astype(BF16)
            t_copy(w, j).start()
        s_copy(w).start()

        def couple(held, top, rows, at, add, tiles=range(4)):
            for u in tiles:
                rhs = held[w, top : top + rows, u * 128 : u * 128 + 128]
                total = None
                for q in range(4):
                    c = u * 4 + q
                    one = dot(bp[c * 96 : c * 96 + 96, at : at + rows], rhs)
                    total = one if total is None else jnp.where(chunk_masks[q], one, total)
                lanes = slice(u * 128, u * 128 + 128)
                cur[:, lanes] = cur[:, lanes] + total if add else total

        for j in range(2):
            t_copy(w, j).wait_send()
        for copy in v_copies(w, 1):
            copy.start()
        s_copy(w).wait_recv()
        couple(tta, 0, 192, 0, False)
        for j in range(2):
            t_copy(w, j).wait_recv()
            f_copy(w, j).start()
        couple(ttb, 0, 96, 256, True)
        for j in range(2):
            f_copy(w, j).wait_recv()

        for up in range(2):
            couple(ttb, 96, 96, 384, True, (2 * up, 2 * up + 1))
            for j in range(12):
                m, ph = j // 6, j % 6
                swapped = [
                    block_swap(cur[j * 8 : j * 8 + 8, u * 128 : u * 128 + 128], masks)
                    for u in (2 * up, 2 * up + 1)
                ]
                at = up * 32 + m * 16
                zz[w, 1, at : at + 16, ph * 128 : ph * 128 + 128] = jnp.concatenate(
                    swapped, axis=0
                ).astype(BF16)
        for up in range(2):
            for copy in z_copies(w, up):
                copy.start()

        for j in range(2):
            if (w, j) != (0, 0):
                for copy in v_copies(w, j):
                    copy.wait_recv()

        def other_links(h, carry):
            for p in range(3):
                _, _, k1, at1, k2, at2 = links[p]
                columns = jnp.concatenate(
                    [win[w][at1 // 3, h, lax.rem(at1, 3)], win[w][at2 // 3, h, lax.rem(at2, 3)]], axis=1
                )
                tiles = jnp.concatenate([off[h, p, k1], off[h, p, k2]], axis=0)
                base[h, p] = base[h, p] - dot(columns, tiles)
            return carry

        lax.fori_loop(0, 16, other_links, 0, unroll=4)

        for up in range(2):
            for copy in z_copies(w, up):
                copy.wait_recv()

        def spread_half(j):
            for p in range(3):
                at = p * 256 + j * 128
                spread[at : at + 128] = lax.dot_general(
                    zz[w, :, :, at : at + 128].reshape(192, 128),
                    hh[...],
                    (((0,), (0,)), ((), ())),
                    preferred_element_type=F32,
                )

        def finish(h, carry):
            hq, e = h // 2, lax.rem(h, 2)
            for p in range(3):
                rows = pl.ds(pl.multiple_of(p * 256 + hq * 32, 32), 32)
                lanes = pl.ds(pl.multiple_of(e * 128, 128), 128)
                residual = (base[h, p] - spread[rows, lanes]).astype(BF16)
                if w == ITERS - 1:
                    resid[h, p] = residual
                else:
                    rounded = dot(residual, inv[h, p]).astype(BF16)
                    vb[w + 1, h, p] = rounded
                    win[w + 1][1, h, p] = rounded
            return carry

        if w < ITERS - 1:
            for j in range(2):
                spread_half(j)
                lax.fori_loop(j * 8, j * 8 + 8, finish, 0, unroll=8)
                pick_half(w + 1, j)
            for copy in v_copies(w + 1, 0):
                copy.start()
        else:
            for j in range(2):
                spread_half(j)
                lax.fori_loop(j * 8, j * 8 + 8, finish, 0, unroll=4)
                results[j].start()

    for w in range(ITERS):
        for j in range(2):
            picks = [] if (w, j) == (0, 0) else x_copies(w, j)
            for copy in v_copies(w, j) + picks + z_copies(w, j):
                copy.wait_send()
            f_copy(w, j).wait_send()
        s_copy(w).wait_send()
    for copy in results:
        copy.wait()


def column_order():
    order = np.full((512,), -100000, np.int32)
    for start in (0, 96, 256, 384):
        for h in range(16):
            for p in range(3):
                for m in range(2):
                    order[start + h * 6 + p * 2 + m] = h * 6 + m * 3 + p
    return np.tile(order[None], (8, 1))


def per_device(n_bus, injection, inv_diag, off_tiles, pattern, coupling, site_map, bus_map):
    smem = pl.BlockSpec(memory_space=pltpu.SMEM)
    hbm = pl.BlockSpec(memory_space=pl.ANY)
    vmem = pl.BlockSpec(memory_space=pltpu.VMEM)
    dma = pltpu.SemaphoreType.DMA
    tiles = (16, 3, 32, 128)
    residual = pl.pallas_call(
        functools.partial(kernel, n_bus),
        out_shape=jax.ShapeDtypeStruct(tiles, BF16),
        in_specs=[smem, smem, smem, vmem, hbm, hbm, hbm, hbm],
        out_specs=hbm,
        scratch_shapes=[
            pltpu.VMEM(tiles, BF16),
            pltpu.VMEM((16, 3, 128, 128), BF16),
            pltpu.VMEM((16, 3, 3, 128, 128), BF16),
            pltpu.VMEM((1536, 384), BF16),
            pltpu.VMEM((384, 512), BF16),
            pltpu.VMEM((1536, 512), BF16),
            pltpu.VMEM((ITERS,) + tiles, BF16),
            pltpu.VMEM((3,) + tiles, BF16),
            pltpu.VMEM((3,) + tiles, BF16),
            pltpu.VMEM((3, 32, 128), jnp.int32),
            pltpu.VMEM((96, 128), BF16),
            pltpu.VMEM((32, 384), BF16),
            pltpu.VMEM((192, 256), BF16),
            pltpu.VMEM(tiles, F32),
            pltpu.VMEM((32, 768), F32),
            pltpu.VMEM((ITERS, 3, 32, 1536), BF16),
            pltpu.VMEM((ITERS, 2, 32, 1536), BF16),
            pltpu.VMEM((ITERS, 192, 512), BF16),
            pltpu.VMEM((ITERS, 192, 512), BF16),
            pltpu.VMEM((96, 512), F32),
            pltpu.VMEM((ITERS, 3, 64, 768), BF16),
            pltpu.VMEM((768, 256), F32),
            pltpu.VMEM(tiles, BF16),
            dma((4,)),
            dma((ITERS, 2, 2)),
            dma((ITERS, 2, 2)),
            dma((ITERS, 2, 2)),
            dma((ITERS, 2, 2)),
            dma((ITERS, 2)),
            dma((ITERS, 2)),
            dma((ITERS, 2)),
            dma((ITERS, 2)),
            dma((ITERS,)),
            dma((ITERS,)),
            dma((ITERS, 2, 2)),
            dma((ITERS, 2, 2)),
            dma((2,)),
            dma((2,)),
            dma((2,)),
        ],
        compiler_params=pltpu.CompilerParams(
            collective_id=0, has_side_effects=True, vmem_limit_bytes=56 << 20
        ),
    )(
        site_map,
        bus_map,
        pattern,
        jnp.asarray(column_order()),
        injection,
        inv_diag,
        off_tiles,
        coupling.reshape(1536, 384),
    )
    last = jnp.einsum(
        "tsa,tab->tsb", residual.reshape(48, 32, 128), inv_diag.reshape(48, 128, 128), preferred_element_type=F32
    )
    return last.reshape(tiles)


def solution(mesh):
    in_specs = (
        P("harm", "bus", None, None),
        P("harm", "bus", None, None),
        P("harm", "bus", None, None, None),
        P("bus", None),
        P("bus", None, "harm", None),
        P("bus"),
        P("bus"),
    )
    out_specs = P("harm", "bus", None, None)
    return jax.shard_map(
        functools.partial(per_device, mesh.shape["bus"]),
        mesh=mesh,
        in_specs=in_specs,
        out_specs=out_specs,
        check_vma=False,
    )
```

```python
import functools

import jax
import jax.numpy as jnp
import numpy as np
from jax import lax
from jax.experimental import pallas as pl
from jax.experimental.pallas import tpu as pltpu
from jax.sharding import PartitionSpec as P

ITERS = 2
MESH = pl.DeviceIdType.MESH
F32 = jnp.float32
BF16 = jnp.bfloat16

V_RUNS = (((0, 8), (8, 16)), ((0, 6), (6, 16)))
HALF_ROWS = 48


def dot(a, b):
    return jnp.dot(a, b, preferred_element_type=F32)


def block_swap(a, masks):
    out = a
    for k in range(1, 4):
        moved = pltpu.roll(pltpu.roll(a, 32 * k, 1), 8 - 2 * k, 0)
        out = jnp.where(masks[k], moved, out)
    return out


def kernel(
    n_bus,
    site_ref, bus_ref, pat_ref, order_ref, inj_hbm, inv_hbm, off_hbm, cpl_hbm,
    out_hbm,
    inj, inv, off, cpl, perm, bp, vb, win_0, win_1, tabs, ehot, wide_hot, hh, base, picked, xs, xr, tta, ttb, cur, zz, spread, resid,
    load_sem, v_send, v_recv, x_send, x_recv, t_send, t_recv, f_send, f_recv, s_send, s_recv, z_send, z_recv, tab_send, tab_recv, out_sem,
):
    win = (win_0, win_1)
    me = lax.axis_index("bus")
    harm = lax.axis_index("harm")
    left = lax.rem(me + n_bus - 1, n_bus)
    right = lax.rem(me + 1, n_bus)
    zh, core = harm // 2, lax.rem(harm, 2)
    to_left, to_right = (left, harm), (right, harm)
    sibling = (me, zh * 2 + 1 - core)
    partner = (me, (1 - zh) * 2 + core)

    loads = [
        pltpu.make_async_copy(src, dst, load_sem.at[i])
        for i, (src, dst) in enumerate(((inj_hbm, inj), (inv_hbm, inv), (cpl_hbm, cpl), (off_hbm, off)))
    ]
    for load in loads:
        load.start()

    barrier = pltpu.get_barrier_semaphore()
    for peer in (to_left, to_right, sibling, partner):
        pl.semaphore_signal(barrier, inc=1, device_id=peer, device_id_type=MESH)

    def remote(src, dst, send, recv, peer):
        return pltpu.make_async_remote_copy(
            src_ref=src, dst_ref=dst, send_sem=send, recv_sem=recv, device_id=peer, device_id_type=MESH
        )

    tab_copies = [
        remote(tabs.at[1], tabs.at[0], tab_send.at[0], tab_recv.at[0], to_right),
        remote(tabs.at[1], tabs.at[2], tab_send.at[1], tab_recv.at[1], to_left),
    ]

    def v_copies(w, j):
        run = pl.ds(V_RUNS[w][j][0], V_RUNS[w][j][1] - V_RUNS[w][j][0])
        return [
            remote(vb.at[w, run], win[w].at[2, run], v_send.at[w, j, 0], v_recv.at[w, j, 0], to_left),
            remote(vb.at[w, run], win[w].at[0, run], v_send.at[w, j, 1], v_recv.at[w, j, 1], to_right),
        ]

    def x_copies(w, j):
        lanes = pl.ds(j * 768, 768)
        return [
            remote(xs.at[w, 0, :, lanes], xr.at[w, 1, :, lanes], x_send.at[w, j, 0], x_recv.at[w, j, 0], to_left),
            remote(xs.at[w, 2, :, lanes], xr.at[w, 0, :, lanes], x_send.at[w, j, 1], x_recv.at[w, j, 1], to_right),
        ]

    def rows_of(j, at):
        return pl.ds(at + j * HALF_ROWS, HALF_ROWS)

    def t_copy(w, j):
        return remote(
            tta.at[w, rows_of(j, 0)], ttb.at[w, rows_of(j, 0)], t_send.at[w, j], t_recv.at[w, j], partner
        )

    def f_copy(w, j):
        return remote(
            ttb.at[w, rows_of(j, 0)], ttb.at[w, rows_of(j, 96)], f_send.at[w, j], f_recv.at[w, j], sibling
        )

    def s_copy(w):
        return remote(tta.at[w, pl.ds(0, 96)], tta.at[w, pl.ds(96, 96)], s_send.at[w], s_recv.at[w], sibling)

    def z_copies(w):
        return [
            remote(zz.at[w, 1], zz.at[w, 2], z_send.at[w, 0], z_recv.at[w, 0], to_left),
            remote(zz.at[w, 1], zz.at[w, 0], z_send.at[w, 1], z_recv.at[w, 1], to_right),
        ]

    conv_row = lax.broadcasted_iota(jnp.int32, (32, 128), 0) // 2
    table = jnp.zeros((32, 128), jnp.int32)
    for c in range(16):
        table = jnp.where(conv_row == c, site_ref[c] * 128 + bus_ref[c], table)
    tabs[1] = table
    parity = lax.rem(lax.broadcasted_iota(jnp.int32, (32, 128), 0), 2)
    lane = lax.broadcasted_iota(jnp.int32, (32, 128), 1)
    for g in range(3):
        hit = (table + parity * 64) == (lane + (me - 1 + g) * 128)
        wide_hot[:, g * 128 : g * 128 + 128] = jnp.where(hit, 1.0, 0.0).astype(BF16)

    loads[0].wait()
    loads[1].wait()

    def first(h, carry):
        for p in range(3):
            rounded = dot(inj[h, p], inv[h, p]).astype(BF16)
            vb[0, h, p] = rounded
            win[0][1, h, p] = rounded
        return carry

    lax.fori_loop(0, 16, first, 0, unroll=4)

    pl.semaphore_wait(barrier, 4)
    for copy in tab_copies + v_copies(0, 0):
        copy.start()

    sub = lax.broadcasted_iota(jnp.int32, (8, 128), 0) // 2
    chunk = lax.broadcasted_iota(jnp.int32, (8, 128), 1) // 32
    shift = lax.rem(chunk - sub + 4, 4)
    masks = [shift == k for k in range(4)]
    chunk96 = lax.broadcasted_iota(jnp.int32, (96, 128), 1) // 32
    chunk_masks = [chunk96 == k for k in range(4)]

    links = []
    for p in range(3):
        at = [pat_ref[p, k] - (me - 1) * 3 for k in range(3)]
        own = [(a >= 3) & (a < 6) for a in at]
        k0 = jnp.where(own[0], 0, jnp.where(own[1], 1, 2))
        k1 = jnp.where(k0 == 0, 1, 0)
        k2 = jnp.where(k0 == 2, 1, 2)

        def pick(k):
            return jnp.where(k == 0, at[0], jnp.where(k == 1, at[1], at[2]))

        links.append((k0, jnp.clip(pick(k0) - 3, 0, 2), k1, jnp.clip(pick(k1), 0, 8), k2, jnp.clip(pick(k2), 0, 8)))

    def pick_half(w, j):
        for part in range(3):
            held = vb[w, j * 8 : j * 8 + 8].reshape(768, 128)[part * 256 : part * 256 + 256]
            got = lax.dot_general(
                ehot[...], held, (((1,), (1,)), ((), ())), preferred_element_type=F32
            ).astype(BF16)
            at = j * 768 + part * 256
            for g in range(3):
                xs[w, g, :, at : at + 256] = got[g * 32 : g * 32 + 32]
        for copy in x_copies(w, j):
            copy.start()

    for copy in tab_copies:
        copy.wait()
    for g in range(3):
        hit = (tabs[g] + parity * 64) == (lane + me * 128)
        ehot[g * 32 : g * 32 + 32] = jnp.where(hit, 1.0, 0.0).astype(BF16)
    pick_half(0, 1)

    row256 = lax.rem(lax.broadcasted_iota(jnp.int32, (16, 256), 0), 2)
    lane256 = lax.broadcasted_iota(jnp.int32, (16, 256), 1)
    bus256 = lax.rem(lane256, 64) + me * 128
    part256 = lane256 // 64
    for g in range(3):
        for up in range(2):
            tab = tabs[g, up * 16 : up * 16 + 16]
            wide = jnp.concatenate([tab, tab], axis=1)
            for m in range(2):
                hit = (wide == bus256) & (part256 == row256 * 2 + m)
                at = g * 64 + up * 32 + m * 16
                hh[at : at + 16] = jnp.where(hit, 1.0, 0.0).astype(BF16)

    col = lax.broadcasted_iota(jnp.int32, (8, 512), 1)
    slot_bits = jnp.where(col < 256, jnp.where(col >= 96, 1, 0), jnp.where(col >= 384, 3, 2))
    source = jnp.bitwise_xor(slot_bits, harm) * 96 + order_ref[...]
    for r in range(48):
        row = lax.broadcasted_iota(jnp.int32, (8, 512), 0) + r * 8
        hot = jnp.where(row == source[0:1], 1.0, 0.0)
        if r % 2 == 0:
            kept = hot
        else:
            perm[(r - 1) * 8 : (r + 1) * 8] = jnp.concatenate([kept, hot], axis=0).astype(BF16)
    loads[2].wait()

    def permute(c, carry):
        rows = pl.ds(pl.multiple_of(c * 96, 96), 96)
        bp[rows] = dot(cpl[rows], perm[...]).astype(BF16)
        return carry

    lax.fori_loop(0, 16, permute, 0)
    loads[3].wait()

    results = []
    for j in range(2):
        half = pl.ds(j * 8, 8)
        results.append(pltpu.make_async_copy(resid.at[half], out_hbm.at[half], out_sem.at[j]))

    for w in range(ITERS):

        def own_links(h, carry):
            for p in range(3):
                k0, own_at = links[p][:2]
                base[h, p] = inj[h, p].astype(F32) - dot(vb[w, h, own_at], off[h, p, k0])
            return carry

        lax.fori_loop(0, 16, own_links, 0, unroll=4)

        for j in range(2):
            if (w, j) == (0, 0):
                for copy in v_copies(0, 0):
                    copy.wait_recv()
                for part in range(3):
                    held = jnp.concatenate(
                        [
                            win[0][g, 0:8].reshape(768, 128)[part * 256 : part * 256 + 256]
                            for g in range(3)
                        ],
                        axis=1,
                    )
                    picked[:, part * 256 : part * 256 + 256] = lax.dot_general(
                        wide_hot[...], held, (((1,), (1,)), ((), ())), preferred_element_type=F32
                    )
            else:
                for copy in x_copies(w, j):
                    copy.wait_recv()
            for tp in range(3 * j, 3 * j + 3):
                for up in range(2):
                    both = []
                    for t in (2 * tp, 2 * tp + 1):
                        rows, lanes = slice(up * 16, up * 16 + 16), slice(t * 128, t * 128 + 128)
                        if (w, j) == (0, 0):
                            both.append(picked[rows, lanes])
                            continue
                        both.append(
                            xs[w, 1, rows, lanes].astype(F32)
                            + xr[w, 0, rows, lanes].astype(F32)
                            + xr[w, 1, rows, lanes].astype(F32)
                        )
                    for half in range(2):
                        u = up * 2 + half
                        swapped = [block_swap(b[half * 8 : half * 8 + 8], masks) for b in both]
                        tta[w, tp * 16 : tp * 16 + 16, u * 128 : u * 128 + 128] = jnp.concatenate(
                            swapped, axis=0
                        ).astype(BF16)
            t_copy(w, j).start()
        s_copy(w).start()

        def couple(held, top, rows, at, add, tiles=range(4)):
            for u in tiles:
                rhs = held[w, top : top + rows, u * 128 : u * 128 + 128]
                total = None
                for q in range(4):
                    c = u * 4 + q
                    one = dot(bp[c * 96 : c * 96 + 96, at : at + rows], rhs)
                    total = one if total is None else jnp.where(chunk_masks[q], one, total)
                lanes = slice(u * 128, u * 128 + 128)
                cur[:, lanes] = cur[:, lanes] + total if add else total

        for j in range(2):
            t_copy(w, j).wait_send()
        for copy in v_copies(w, 1):
            copy.start()
        s_copy(w).wait_recv()
        couple(tta, 0, 192, 0, False)
        for j in range(2):
            t_copy(w, j).wait_recv()
            f_copy(w, j).start()
        couple(ttb, 0, 96, 256, True)
        for j in range(2):
            f_copy(w, j).wait_recv()

        for up in range(2):
            couple(ttb, 96, 96, 384, True, (2 * up, 2 * up + 1))
            for j in range(12):
                m, ph = j // 6, j % 6
                swapped = [
                    block_swap(cur[j * 8 : j * 8 + 8, u * 128 : u * 128 + 128], masks)
                    for u in (2 * up, 2 * up + 1)
                ]
                at = up * 32 + m * 16
                zz[w, 1, at : at + 16, ph * 128 : ph * 128 + 128] = jnp.concatenate(
                    swapped, axis=0
                ).astype(BF16)
        for copy in z_copies(w):
            copy.start()

        for j in range(2):
            if (w, j) != (0, 0):
                for copy in v_copies(w, j):
                    copy.wait_recv()

        def other_links(h, carry):
            for p in range(3):
                _, _, k1, at1, k2, at2 = links[p]
                columns = jnp.concatenate(
                    [win[w][at1 // 3, h, lax.rem(at1, 3)], win[w][at2 // 3, h, lax.rem(at2, 3)]], axis=1
                )
                tiles = jnp.concatenate([off[h, p, k1], off[h, p, k2]], axis=0)
                base[h, p] = base[h, p] - dot(columns, tiles)
            return carry

        lax.fori_loop(0, 16, other_links, 0, unroll=4)

        for copy in z_copies(w):
            copy.wait_recv()

        def spread_half(j):
            for p in range(3):
                at = p * 256 + j * 128
                spread[at : at + 128] = lax.dot_general(
                    zz[w, :, :, at : at + 128].reshape(192, 128),
                    hh[...],
                    (((0,), (0,)), ((), ())),
                    preferred_element_type=F32,
                )

        def finish(h, carry):
            hq, e = h // 2, lax.rem(h, 2)
            for p in range(3):
                rows = pl.ds(pl.multiple_of(p * 256 + hq * 32, 32), 32)
                lanes = pl.ds(pl.multiple_of(e * 128, 128), 128)
                residual = (base[h, p] - spread[rows, lanes]).astype(BF16)
                if w == ITERS - 1:
                    resid[h, p] = residual
                else:
                    rounded = dot(residual, inv[h, p]).astype(BF16)
                    vb[w + 1, h, p] = rounded
                    win[w + 1][1, h, p] = rounded
            return carry

        if w < ITERS - 1:
            for j in range(2):
                spread_half(j)
                lax.fori_loop(j * 8, j * 8 + 8, finish, 0, unroll=8)
                pick_half(w + 1, j)
            for copy in v_copies(w + 1, 0):
                copy.start()
        else:
            for j in range(2):
                spread_half(j)
                lax.fori_loop(j * 8, j * 8 + 8, finish, 0, unroll=4)
                results[j].start()

    for w in range(ITERS):
        for j in range(2):
            picks = [] if (w, j) == (0, 0) else x_copies(w, j)
            for copy in v_copies(w, j) + picks:
                copy.wait_send()
            f_copy(w, j).wait_send()
        for copy in z_copies(w) + [s_copy(w)]:
            copy.wait_send()
    for copy in results:
        copy.wait()


def column_order():
    order = np.full((512,), -100000, np.int32)
    for start in (0, 96, 256, 384):
        for h in range(16):
            for p in range(3):
                for m in range(2):
                    order[start + h * 6 + p * 2 + m] = h * 6 + m * 3 + p
    return np.tile(order[None], (8, 1))


def per_device(n_bus, injection, inv_diag, off_tiles, pattern, coupling, site_map, bus_map):
    smem = pl.BlockSpec(memory_space=pltpu.SMEM)
    hbm = pl.BlockSpec(memory_space=pl.ANY)
    vmem = pl.BlockSpec(memory_space=pltpu.VMEM)
    dma = pltpu.SemaphoreType.DMA
    tiles = (16, 3, 32, 128)
    residual = pl.pallas_call(
        functools.partial(kernel, n_bus),
        out_shape=jax.ShapeDtypeStruct(tiles, BF16),
        in_specs=[smem, smem, smem, vmem, hbm, hbm, hbm, hbm],
        out_specs=hbm,
        scratch_shapes=[
            pltpu.VMEM(tiles, BF16),
            pltpu.VMEM((16, 3, 128, 128), BF16),
            pltpu.VMEM((16, 3, 3, 128, 128), BF16),
            pltpu.VMEM((1536, 384), BF16),
            pltpu.VMEM((384, 512), BF16),
            pltpu.VMEM((1536, 512), BF16),
            pltpu.VMEM((ITERS,) + tiles, BF16),
            pltpu.VMEM((3,) + tiles, BF16),
            pltpu.VMEM((3,) + tiles, BF16),
            pltpu.VMEM((3, 32, 128), jnp.int32),
            pltpu.VMEM((96, 128), BF16),
            pltpu.VMEM((32, 384), BF16),
            pltpu.VMEM((192, 256), BF16),
            pltpu.VMEM(tiles, F32),
            pltpu.VMEM((32, 768), F32),
            pltpu.VMEM((ITERS, 3, 32, 1536), BF16),
            pltpu.VMEM((ITERS, 2, 32, 1536), BF16),
            pltpu.VMEM((ITERS, 192, 512), BF16),
            pltpu.VMEM((ITERS, 192, 512), BF16),
            pltpu.VMEM((96, 512), F32),
            pltpu.VMEM((ITERS, 3, 64, 768), BF16),
            pltpu.VMEM((768, 256), F32),
            pltpu.VMEM(tiles, BF16),
            dma((4,)),
            dma((ITERS, 2, 2)),
            dma((ITERS, 2, 2)),
            dma((ITERS, 2, 2)),
            dma((ITERS, 2, 2)),
            dma((ITERS, 2)),
            dma((ITERS, 2)),
            dma((ITERS, 2)),
            dma((ITERS, 2)),
            dma((ITERS,)),
            dma((ITERS,)),
            dma((ITERS, 2)),
            dma((ITERS, 2)),
            dma((2,)),
            dma((2,)),
            dma((2,)),
        ],
        compiler_params=pltpu.CompilerParams(
            collective_id=0, has_side_effects=True, vmem_limit_bytes=56 << 20
        ),
    )(
        site_map,
        bus_map,
        pattern,
        jnp.asarray(column_order()),
        injection,
        inv_diag,
        off_tiles,
        coupling.reshape(1536, 384),
    )
    last = jnp.einsum(
        "tsa,tab->tsb", residual.reshape(48, 32, 128), inv_diag.reshape(48, 128, 128), preferred_element_type=F32
    )
    return last.reshape(tiles)


def solution(mesh):
    in_specs = (
        P("harm", "bus", None, None),
        P("harm", "bus", None, None),
        P("harm", "bus", None, None, None),
        P("bus", None),
        P("bus", None, "harm", None),
        P("bus"),
        P("bus"),
    )
    out_specs = P("harm", "bus", None, None)
    return jax.shard_map(
        functools.partial(per_device, mesh.shape["bus"]),
        mesh=mesh,
        in_specs=in_specs,
        out_specs=out_specs,
        check_vma=False,
    )
```

```python
import functools

import jax
import jax.numpy as jnp
import numpy as np
from jax import lax
from jax.experimental import pallas as pl
from jax.experimental.pallas import tpu as pltpu
from jax.sharding import PartitionSpec as P

ITERS = 2
MESH = pl.DeviceIdType.MESH
F32 = jnp.float32
BF16 = jnp.bfloat16

V_RUNS = (((0, 8), (8, 16)), ((0, 6), (6, 16)))
HALF_ROWS = 48


def dot(a, b):
    return jnp.dot(a, b, preferred_element_type=F32)


def block_swap(a, masks):
    out = a
    for k in range(1, 4):
        moved = pltpu.roll(pltpu.roll(a, 32 * k, 1), 8 - 2 * k, 0)
        out = jnp.where(masks[k], moved, out)
    return out


def kernel(
    n_bus,
    site_ref, bus_ref, pat_ref, order_ref, inj_hbm, inv_hbm, off_hbm, cpl_hbm,
    out_hbm,
    inj, inv, off, cpl, perm, bp, vb, win_0, win_1, tabs, ehot, wide_hot, hh, base, picked, xs, xr, tta, ttb, cur, zz, spread, resid,
    load_sem, v_send, v_recv, x_send, x_recv, t_send, t_recv, f_send, f_recv, s_send, s_recv, z_send, z_recv, tab_send, tab_recv, out_sem,
):
    win = (win_0, win_1)
    me = lax.axis_index("bus")
    harm = lax.axis_index("harm")
    left = lax.rem(me + n_bus - 1, n_bus)
    right = lax.rem(me + 1, n_bus)
    zh, core = harm // 2, lax.rem(harm, 2)
    to_left, to_right = (left, harm), (right, harm)
    sibling = (me, zh * 2 + 1 - core)
    partner = (me, (1 - zh) * 2 + core)

    loads = [
        pltpu.make_async_copy(src, dst, load_sem.at[i])
        for i, (src, dst) in enumerate(((inj_hbm, inj), (inv_hbm, inv), (cpl_hbm, cpl), (off_hbm, off)))
    ]
    for load in loads:
        load.start()

    barrier = pltpu.get_barrier_semaphore()
    for peer in (to_left, to_right, sibling, partner):
        pl.semaphore_signal(barrier, inc=1, device_id=peer, device_id_type=MESH)

    def remote(src, dst, send, recv, peer):
        return pltpu.make_async_remote_copy(
            src_ref=src, dst_ref=dst, send_sem=send, recv_sem=recv, device_id=peer, device_id_type=MESH
        )

    tab_copies = [
        remote(tabs.at[1], tabs.at[0], tab_send.at[0], tab_recv.at[0], to_right),
        remote(tabs.at[1], tabs.at[2], tab_send.at[1], tab_recv.at[1], to_left),
    ]

    def v_copies(w, j):
        run = pl.ds(V_RUNS[w][j][0], V_RUNS[w][j][1] - V_RUNS[w][j][0])
        return [
            remote(vb.at[w, run], win[w].at[2, run], v_send.at[w, j, 0], v_recv.at[w, j, 0], to_left),
            remote(vb.at[w, run], win[w].at[0, run], v_send.at[w, j, 1], v_recv.at[w, j, 1], to_right),
        ]

    def x_copies(w, j):
        lanes = pl.ds(j * 768, 768)
        return [
            remote(xs.at[w, 0, :, lanes], xr.at[w, 1, :, lanes], x_send.at[w, j, 0], x_recv.at[w, j, 0], to_left),
            remote(xs.at[w, 2, :, lanes], xr.at[w, 0, :, lanes], x_send.at[w, j, 1], x_recv.at[w, j, 1], to_right),
        ]

    def rows_of(j, at):
        return pl.ds(at + j * HALF_ROWS, HALF_ROWS)

    def t_copy(w, j):
        return remote(
            tta.at[w, rows_of(j, 0)], ttb.at[w, rows_of(j, 0)], t_send.at[w, j], t_recv.at[w, j], partner
        )

    def f_copy(w, j):
        return remote(
            ttb.at[w, rows_of(j, 0)], ttb.at[w, rows_of(j, 96)], f_send.at[w, j], f_recv.at[w, j], sibling
        )

    def s_copy(w):
        return remote(tta.at[w, pl.ds(0, 96)], tta.at[w, pl.ds(96, 96)], s_send.at[w], s_recv.at[w], sibling)

    def z_copies(w):
        return [
            remote(zz.at[w, 1], zz.at[w, 2], z_send.at[w, 0], z_recv.at[w, 0], to_left),
            remote(zz.at[w, 1], zz.at[w, 0], z_send.at[w, 1], z_recv.at[w, 1], to_right),
        ]

    conv_row = lax.broadcasted_iota(jnp.int32, (32, 128), 0) // 2
    table = jnp.zeros((32, 128), jnp.int32)
    for c in range(16):
        table = jnp.where(conv_row == c, site_ref[c] * 128 + bus_ref[c], table)
    tabs[1] = table
    parity = lax.rem(lax.broadcasted_iota(jnp.int32, (32, 128), 0), 2)
    lane = lax.broadcasted_iota(jnp.int32, (32, 128), 1)
    for g in range(3):
        hit = (table + parity * 64) == (lane + (me - 1 + g) * 128)
        wide_hot[:, g * 128 : g * 128 + 128] = jnp.where(hit, 1.0, 0.0).astype(BF16)

    loads[0].wait()
    loads[1].wait()

    def first(h, carry):
        for p in range(3):
            rounded = dot(inj[h, p], inv[h, p]).astype(BF16)
            vb[0, h, p] = rounded
            win[0][1, h, p] = rounded
        return carry

    lax.fori_loop(0, 16, first, 0, unroll=4)

    pl.semaphore_wait(barrier, 4)
    for copy in tab_copies + v_copies(0, 0):
        copy.start()

    sub = lax.broadcasted_iota(jnp.int32, (8, 128), 0) // 2
    chunk = lax.broadcasted_iota(jnp.int32, (8, 128), 1) // 32
    shift = lax.rem(chunk - sub + 4, 4)
    masks = [shift == k for k in range(4)]
    chunk96 = lax.broadcasted_iota(jnp.int32, (96, 128), 1) // 32
    chunk_masks = [chunk96 == k for k in range(4)]

    links = []
    for p in range(3):
        at = [pat_ref[p, k] - (me - 1) * 3 for k in range(3)]
        own = [(a >= 3) & (a < 6) for a in at]
        k0 = jnp.where(own[0], 0, jnp.where(own[1], 1, 2))
        k1 = jnp.where(k0 == 0, 1, 0)
        k2 = jnp.where(k0 == 2, 1, 2)

        def pick(k):
            return jnp.where(k == 0, at[0], jnp.where(k == 1, at[1], at[2]))

        links.append((k0, jnp.clip(pick(k0) - 3, 0, 2), k1, jnp.clip(pick(k1), 0, 8), k2, jnp.clip(pick(k2), 0, 8)))

    def pick_half(w, j):
        for part in range(3):
            held = vb[w, j * 8 : j * 8 + 8].reshape(768, 128)[part * 256 : part * 256 + 256]
            got = lax.dot_general(
                ehot[...], held, (((1,), (1,)), ((), ())), preferred_element_type=F32
            ).astype(BF16)
            at = j * 768 + part * 256
            for g in range(3):
                xs[w, g, :, at : at + 256] = got[g * 32 : g * 32 + 32]
        for copy in x_copies(w, j):
            copy.start()

    for copy in tab_copies:
        copy.wait()
    for g in range(3):
        hit = (tabs[g] + parity * 64) == (lane + me * 128)
        ehot[g * 32 : g * 32 + 32] = jnp.where(hit, 1.0, 0.0).astype(BF16)
    pick_half(0, 1)

    row256 = lax.rem(lax.broadcasted_iota(jnp.int32, (16, 256), 0), 2)
    lane256 = lax.broadcasted_iota(jnp.int32, (16, 256), 1)
    bus256 = lax.rem(lane256, 64) + me * 128
    part256 = lane256 // 64
    for g in range(3):
        for up in range(2):
            tab = tabs[g, up * 16 : up * 16 + 16]
            wide = jnp.concatenate([tab, tab], axis=1)
            for m in range(2):
                hit = (wide == bus256) & (part256 == row256 * 2 + m)
                at = g * 64 + up * 32 + m * 16
                hh[at : at + 16] = jnp.where(hit, 1.0, 0.0).astype(BF16)

    col = lax.broadcasted_iota(jnp.int32, (8, 512), 1)
    slot_bits = jnp.where(col < 256, jnp.where(col >= 96, 1, 0), jnp.where(col >= 384, 3, 2))
    source = jnp.bitwise_xor(slot_bits, harm) * 96 + order_ref[...]
    for r in range(48):
        row = lax.broadcasted_iota(jnp.int32, (8, 512), 0) + r * 8
        hot = jnp.where(row == source[0:1], 1.0, 0.0)
        if r % 2 == 0:
            kept = hot
        else:
            perm[(r - 1) * 8 : (r + 1) * 8] = jnp.concatenate([kept, hot], axis=0).astype(BF16)
    loads[2].wait()

    def permute(c, carry):
        rows = pl.ds(pl.multiple_of(c * 96, 96), 96)
        bp[rows] = dot(cpl[rows], perm[...]).astype(BF16)
        return carry

    lax.fori_loop(0, 16, permute, 0)
    loads[3].wait()

    results = []
    for j in range(2):
        half = pl.ds(j * 8, 8)
        results.append(pltpu.make_async_copy(resid.at[half], out_hbm.at[half], out_sem.at[j]))

    for w in range(ITERS):

        def own_links(h, carry):
            for p in range(3):
                k0, own_at = links[p][:2]
                base[h, p] = inj[h, p].astype(F32) - dot(vb[w, h, own_at], off[h, p, k0])
            return carry

        lax.fori_loop(0, 16, own_links, 0, unroll=4)

        for j in range(2):
            if (w, j) == (0, 0):
                for copy in v_copies(0, 0):
                    copy.wait_recv()
                for part in range(3):
                    held = jnp.concatenate(
                        [
                            win[0][g, 0:8].reshape(768, 128)[part * 256 : part * 256 + 256]
                            for g in range(3)
                        ],
                        axis=1,
                    )
                    picked[:, part * 256 : part * 256 + 256] = lax.dot_general(
                        wide_hot[...], held, (((1,), (1,)), ((), ())), preferred_element_type=F32
                    )
            else:
                for copy in x_copies(w, j):
                    copy.wait_recv()
            for tp in range(3 * j, 3 * j + 3):
                for up in range(2):
                    both = []
                    for t in (2 * tp, 2 * tp + 1):
                        rows, lanes = slice(up * 16, up * 16 + 16), slice(t * 128, t * 128 + 128)
                        if (w, j) == (0, 0):
                            both.append(picked[rows, lanes])
                            continue
                        both.append(
                            xs[w, 1, rows, lanes].astype(F32)
                            + xr[w, 0, rows, lanes].astype(F32)
                            + xr[w, 1, rows, lanes].astype(F32)
                        )
                    for half in range(2):
                        u = up * 2 + half
                        swapped = [block_swap(b[half * 8 : half * 8 + 8], masks) for b in both]
                        tta[w, tp * 16 : tp * 16 + 16, u * 128 : u * 128 + 128] = jnp.concatenate(
                            swapped, axis=0
                        ).astype(BF16)
            t_copy(w, j).start()
        s_copy(w).start()

        def couple(held, top, rows, at, add, tiles=range(4)):
            for u in tiles:
                rhs = held[w, top : top + rows, u * 128 : u * 128 + 128]
                total = None
                for q in range(4):
                    c = u * 4 + q
                    one = dot(bp[c * 96 : c * 96 + 96, at : at + rows], rhs)
                    total = one if total is None else jnp.where(chunk_masks[q], one, total)
                lanes = slice(u * 128, u * 128 + 128)
                cur[:, lanes] = cur[:, lanes] + total if add else total

        for j in range(2):
            t_copy(w, j).wait_send()
        for copy in v_copies(w, 1):
            copy.start()
        s_copy(w).wait_recv()
        couple(tta, 0, 192, 0, False)
        for j in range(2):
            t_copy(w, j).wait_recv()
            f_copy(w, j).start()
        couple(ttb, 0, 96, 256, True)
        for j in range(2):
            f_copy(w, j).wait_recv()

        for up in range(2):
            couple(ttb, 96, 96, 384, True, (2 * up, 2 * up + 1))
            for j in range(12):
                m, ph = j // 6, j % 6
                swapped = [
                    block_swap(cur[j * 8 : j * 8 + 8, u * 128 : u * 128 + 128], masks)
                    for u in (2 * up, 2 * up + 1)
                ]
                at = up * 32 + m * 16
                zz[w, 1, at : at + 16, ph * 128 : ph * 128 + 128] = jnp.concatenate(
                    swapped, axis=0
                ).astype(BF16)
        for copy in z_copies(w):
            copy.start()

        for j in range(2):
            if (w, j) != (0, 0):
                for copy in v_copies(w, j):
                    copy.wait_recv()

        def other_links(h, carry):
            for p in range(3):
                _, _, k1, at1, k2, at2 = links[p]
                columns = jnp.concatenate(
                    [win[w][at1 // 3, h, lax.rem(at1, 3)], win[w][at2 // 3, h, lax.rem(at2, 3)]], axis=1
                )
                tiles = jnp.concatenate([off[h, p, k1], off[h, p, k2]], axis=0)
                base[h, p] = base[h, p] - dot(columns, tiles)
            return carry

        lax.fori_loop(0, 16, other_links, 0, unroll=4)

        for copy in z_copies(w):
            copy.wait_recv()

        def spread_half(j):
            for p in range(3):
                at = p * 256 + j * 128
                spread[at : at + 128] = lax.dot_general(
                    zz[w, :, :, at : at + 128].reshape(192, 128),
                    hh[...],
                    (((0,), (0,)), ((), ())),
                    preferred_element_type=F32,
                )

        def finish(h, carry):
            hq, e = h // 2, lax.rem(h, 2)
            for p in range(3):
                rows = pl.ds(pl.multiple_of(p * 256 + hq * 32, 32), 32)
                lanes = pl.ds(pl.multiple_of(e * 128, 128), 128)
                residual = (base[h, p] - spread[rows, lanes]).astype(BF16)
                if w == ITERS - 1:
                    resid[h, p] = residual
                else:
                    rounded = dot(residual, inv[h, p]).astype(BF16)
                    vb[w + 1, h, p] = rounded
                    win[w + 1][1, h, p] = rounded
            return carry

        if w < ITERS - 1:
            for j in range(2):
                spread_half(j)
                lax.fori_loop(j * 8, j * 8 + 8, finish, 0, unroll=8)
                pick_half(w + 1, j)
            for copy in v_copies(w + 1, 0):
                copy.start()
        else:
            for j in range(2):
                spread_half(j)
                lax.fori_loop(j * 8, j * 8 + 8, finish, 0, unroll=8)
                results[j].start()

    for w in range(ITERS):
        for j in range(2):
            picks = [] if (w, j) == (0, 0) else x_copies(w, j)
            for copy in v_copies(w, j) + picks:
                copy.wait_send()
            f_copy(w, j).wait_send()
        for copy in z_copies(w) + [s_copy(w)]:
            copy.wait_send()
    for copy in results:
        copy.wait()


def column_order():
    order = np.full((512,), -100000, np.int32)
    for start in (0, 96, 256, 384):
        for h in range(16):
            for p in range(3):
                for m in range(2):
                    order[start + h * 6 + p * 2 + m] = h * 6 + m * 3 + p
    return np.tile(order[None], (8, 1))


def per_device(n_bus, injection, inv_diag, off_tiles, pattern, coupling, site_map, bus_map):
    smem = pl.BlockSpec(memory_space=pltpu.SMEM)
    hbm = pl.BlockSpec(memory_space=pl.ANY)
    vmem = pl.BlockSpec(memory_space=pltpu.VMEM)
    dma = pltpu.SemaphoreType.DMA
    tiles = (16, 3, 32, 128)
    residual = pl.pallas_call(
        functools.partial(kernel, n_bus),
        out_shape=jax.ShapeDtypeStruct(tiles, BF16),
        in_specs=[smem, smem, smem, vmem, hbm, hbm, hbm, hbm],
        out_specs=hbm,
        scratch_shapes=[
            pltpu.VMEM(tiles, BF16),
            pltpu.VMEM((16, 3, 128, 128), BF16),
            pltpu.VMEM((16, 3, 3, 128, 128), BF16),
            pltpu.VMEM((1536, 384), BF16),
            pltpu.VMEM((384, 512), BF16),
            pltpu.VMEM((1536, 512), BF16),
            pltpu.VMEM((ITERS,) + tiles, BF16),
            pltpu.VMEM((3,) + tiles, BF16),
            pltpu.VMEM((3,) + tiles, BF16),
            pltpu.VMEM((3, 32, 128), jnp.int32),
            pltpu.VMEM((96, 128), BF16),
            pltpu.VMEM((32, 384), BF16),
            pltpu.VMEM((192, 256), BF16),
            pltpu.VMEM(tiles, F32),
            pltpu.VMEM((32, 768), F32),
            pltpu.VMEM((ITERS, 3, 32, 1536), BF16),
            pltpu.VMEM((ITERS, 2, 32, 1536), BF16),
            pltpu.VMEM((ITERS, 192, 512), BF16),
            pltpu.VMEM((ITERS, 192, 512), BF16),
            pltpu.VMEM((96, 512), F32),
            pltpu.VMEM((ITERS, 3, 64, 768), BF16),
            pltpu.VMEM((768, 256), F32),
            pltpu.VMEM(tiles, BF16),
            dma((4,)),
            dma((ITERS, 2, 2)),
            dma((ITERS, 2, 2)),
            dma((ITERS, 2, 2)),
            dma((ITERS, 2, 2)),
            dma((ITERS, 2)),
            dma((ITERS, 2)),
            dma((ITERS, 2)),
            dma((ITERS, 2)),
            dma((ITERS,)),
            dma((ITERS,)),
            dma((ITERS, 2)),
            dma((ITERS, 2)),
            dma((2,)),
            dma((2,)),
            dma((2,)),
        ],
        compiler_params=pltpu.CompilerParams(
            collective_id=0, has_side_effects=True, vmem_limit_bytes=56 << 20
        ),
    )(
        site_map,
        bus_map,
        pattern,
        jnp.asarray(column_order()),
        injection,
        inv_diag,
        off_tiles,
        coupling.reshape(1536, 384),
    )
    last = jnp.einsum(
        "tsa,tab->tsb", residual.reshape(48, 32, 128), inv_diag.reshape(48, 128, 128), preferred_element_type=F32
    )
    return last.reshape(tiles)


def solution(mesh):
    in_specs = (
        P("harm", "bus", None, None),
        P("harm", "bus", None, None),
        P("harm", "bus", None, None, None),
        P("bus", None),
        P("bus", None, "harm", None),
        P("bus"),
        P("bus"),
    )
    out_specs = P("harm", "bus", None, None)
    return jax.shard_map(
        functools.partial(per_device, mesh.shape["bus"]),
        mesh=mesh,
        in_specs=in_specs,
        out_specs=out_specs,
        check_vma=False,
    )
```
